256 devices in a mesh: ctx: 8 (over z_lo, core), dp: 32 (over z_hi, y, x).
Axes of the slice: x: 4, y: 4, z: 8 (z_hi: 2, z_lo: 4; z = z_hi * 4 + z_lo), core: 2. Of those that a mesh axis runs over, the one named last changes fastest.
Arguments:
- inputs: bfloat16 [32, 1024, 2048], P('dp', 'ctx'), may hold values from -12 to 12
- values: bfloat16 [32, 1024, 2048], P('dp', 'ctx'), may hold values from -6 to 6
- gating: bfloat16 [32, 1024, 2048], P('dp', 'ctx'), may hold values from -6 to 6
- out_grad: bfloat16 [32, 1024, 2048], P('dp', 'ctx'), may hold values from -6 to 6
- weight: bfloat16 [2048, 2048], P('dp'), may hold values from -0.125 to 0.125
- decay_rate: float32 [16, 2048], replicated, may hold values from 0.00048828125 to 0.08
- mode_gain: float32 [16, 2048], replicated, may hold values from -1.75 to 1.75
Outputs:
- in_grad: float32 [32, 1024, 2048], P('dp', 'ctx')
- gate_grad: float32 [32, 1024, 2048], P('dp', 'ctx')
- weight_grad: float32 [2048, 2048], P('dp')
The draws below stay inside these ranges and needn't reach their ends.
All inputs are finite; a program needn't handle non-finite values.
Results may differ from the reference program's by a relative error of at most 0.003.
Values may be sent and summed in bfloat16 or wider, within the bound.
No kernel may reach another device: no remote copies, remote signals or barrier semaphores. Data moves between devices by JAX's collectives and lax.ppermute only.
A program may use at most 128 MiB of HBM per device.

```python
import math
import jax
import jax.numpy as jnp
from jax import lax

D = 2048
C = 2048
MODES = 16
SEQ = 1024
SEQS = 32


def spiked(values, own_key, source, target, parts, factor):
    def block_of(axis_at):
        return (jnp.arange(values.shape[axis_at]) // (values.shape[axis_at] // parts)).reshape((-1,) + (1,) * (values.ndim - 1 - axis_at))

    first = jax.random.permutation(own_key, parts)[block_of(target)]
    second = (block_of(target) + parts // 2) % parts
    return jnp.where((block_of(source) == first) | (block_of(source) == second), factor * values, values)


def steps_of(rng, dims, pieces, least, largest):
    level = 1.0
    for axis_at, blocks in pieces:
        steps = jax.random.uniform(jax.random.fold_in(jax.random.fold_in(rng, 6), axis_at), (blocks,), jnp.float32, least / len(pieces), largest / len(pieces))
        level = level * jnp.repeat(jnp.exp(steps), dims[axis_at] // blocks).reshape((-1,) + (1,) * (len(dims) - 1 - axis_at))
    return level


def scatter_about(rng, extent, width, bound, split=(), dtype=jnp.bfloat16):
    drawn = width * jax.random.normal(rng, extent, jnp.float32)
    if split:
        drawn = drawn * steps_of(rng, extent, split, -0.22, 0.18)
    return jnp.clip(drawn, -bound, bound).astype(dtype)


def gaussian_with(stream_key, dims, width, most, shards, heavy, dtype=jnp.bfloat16):
    values = width * jax.random.normal(stream_key, dims, jnp.float32)
    if shards:
        values = values * steps_of(stream_key, dims, shards, -0.22, 0.18)
    return jnp.clip(spiked(values, jax.random.fold_in(stream_key, 3), *heavy), -most, most).astype(dtype)


def setup_inputs(seed: int = 0) -> dict:
    streams_of = jax.random.split(jax.random.key(seed), 8)
    return {
        "inputs": gaussian_with(streams_of[0], (SEQS, SEQ, D), 1.0, 12.0, ((0, 32), (1, 8)), (0, 2, 32, 2.75)),
        "values": scatter_about(streams_of[1], (SEQS, SEQ, C), 1.0, 6.0, ((0, 32), (1, 8))),
        "gating": scatter_about(streams_of[2], (SEQS, SEQ, C), 1.0, 6.0, ((0, 32), (1, 8))),
        "out_grad": scatter_about(streams_of[3], (SEQS, SEQ, C), 1.0, 6.0, ((0, 32), (1, 8))),
        "weight": scatter_about(streams_of[4], (D, C), C ** -0.5, 0.125, ((0, 32),)),
        "decay_rate": jnp.clip(jnp.exp(jax.random.uniform(streams_of[5], (MODES, C), jnp.float32, math.log(0.00048828125), math.log(0.08))), 0.00048828125, 0.08),
        "mode_gain": scatter_about(streams_of[6], (MODES, C), 0.3, 1.75, (), jnp.float32),
    }


def modal_scan(series, lam, mode_coef, reverse):

    def advance(state, column):
        state = lam[None] * state + column[:, None, :]
        return (state, lax.optimization_barrier(jnp.sum(mode_coef[None] * state, axis=1)))
    initial = jnp.zeros((series.shape[0],) + lam.shape, jnp.float32)
    _, result = lax.scan(advance, initial, jnp.swapaxes(series, 0, 1), reverse=reverse)
    return jnp.swapaxes(result, 0, 1)

def reference(inputs, values, gating, out_grad, weight, decay_rate, mode_gain):
    lam = jnp.exp(-decay_rate)
    mode_coef = mode_gain * jnp.sqrt(-jnp.expm1(-2.0 * decay_rate))
    mixed = modal_scan(values.astype(jnp.float32), lam, mode_coef, False)
    gate_grad = out_grad.astype(jnp.float32) * mixed
    mix_grad = gating.astype(jnp.float32) * out_grad.astype(jnp.float32)
    val_grad = modal_scan(mix_grad, lam, mode_coef, True).astype(jnp.bfloat16)
    flat_grad = val_grad.reshape(-1, C).astype(jnp.float32)
    flat_in = inputs.reshape(-1, D).astype(jnp.float32)
    weight_full = weight.astype(jnp.float32)
    in_grad = lax.dot_general(flat_grad, weight_full, (((1,), (1,)), ((), ())), precision=lax.Precision.HIGHEST, preferred_element_type=jnp.float32)
    in_grad = in_grad.reshape(SEQS, SEQ, D)
    weight_grad = lax.dot_general(flat_in, flat_grad, (((0,), (0,)), ((), ())), precision=lax.Precision.HIGHEST, preferred_element_type=jnp.float32)
    weight_grad = weight_grad / jnp.sqrt(jnp.float32(SEQS * SEQ))
    return (in_grad, gate_grad, weight_grad)
```

```python
import math

import jax
import jax.numpy as jnp
from jax import lax
from jax.experimental import pallas as pl
from jax.experimental.pallas import tpu as pltpu
from jax.sharding import Mesh, PartitionSpec as P

F32 = jnp.float32
BF16 = jnp.bfloat16
LANES = 128
ROWS = 16
CTX = ("zl", "co")
DP = ("zh", "y", "x")


def states_kernel(v_ref, g_ref, o_ref, lam_ref, d16_ref, s_ref, st_ref, xs, us):
    tok, width = v_ref.shape
    modes = lam_ref.shape[0]
    nb = tok // ROWS
    half = modes * nb

    def chunk(j, carry):
        c = pl.ds(pl.multiple_of(j * LANES, LANES), LANES)
        base = pl.multiple_of(j * 2 * half, 2 * half)
        xs[...] = v_ref[:, c].astype(F32)
        us[...] = g_ref[:, c].astype(F32) * o_ref[:, c].astype(F32)
        x = [xs[pl.ds(r, nb, stride=ROWS), :] for r in range(ROWS)]
        u = [us[pl.ds(r, nb, stride=ROWS), :] for r in range(ROWS)]
        for m in range(modes):
            lam = jnp.broadcast_to(lam_ref[pl.ds(m, 1), c], (nb, LANES))
            s = x[0]
            b = u[ROWS - 1]
            for r in range(1, ROWS):
                s = s * lam + x[r]
                b = b * lam + u[ROWS - 1 - r]
            s_ref[pl.ds(base + m * nb, nb), :] = s
            s_ref[pl.ds(base + half + m * nb, nb), :] = b
        d16 = d16_ref[:, c]
        f = s_ref[pl.ds(base, modes, stride=nb), :]
        b = s_ref[pl.ds(base + half + nb - 1, modes, stride=nb), :]
        for i in range(1, nb):
            f = f * d16 + s_ref[pl.ds(base + i, modes, stride=nb), :]
            b = b * d16 + s_ref[pl.ds(base + half + nb - 1 - i, modes, stride=nb), :]
        st_ref[0:modes, c] = f
        st_ref[modes : 2 * modes, c] = b
        return carry

    lax.fori_loop(0, width // LANES, chunk, 0)


def outputs_kernel(
    v_ref, g_ref, o_ref, lam_ref, d16_ref, coef_ref, h_ref, s_ref, in_ref, gate_ref, vg_ref, xs, us, ps
):
    tok, width = v_ref.shape
    modes = lam_ref.shape[0]
    nb = tok // ROWS
    half = modes * nb

    def chunk(j, carry):
        c = pl.ds(pl.multiple_of(j * LANES, LANES), LANES)
        base = pl.multiple_of(j * 2 * half, 2 * half)
        grad = o_ref[:, c].astype(F32)
        xs[...] = v_ref[:, c].astype(F32)
        us[...] = g_ref[:, c].astype(F32) * grad
        d16 = d16_ref[:, c]
        coef = coef_ref[:, c]
        f = in_ref[0:modes, c]
        b = in_ref[modes : 2 * modes, c]
        for i in range(nb):
            ps[pl.ds(i, modes, stride=nb), :] = f * coef
            ps[pl.ds(half + nb - 1 - i, modes, stride=nb), :] = b * coef
            if i < nb - 1:
                f = f * d16 + s_ref[pl.ds(base + i, modes, stride=nb), :]
                b = b * d16 + s_ref[pl.ds(base + half + nb - 1 - i, modes, stride=nb), :]
        for back in range(2):
            src = us if back else xs
            x = [src[pl.ds(r, nb, stride=ROWS), :] for r in range(ROWS)]
            if back:
                x = x[::-1]
            y = [None] * ROWS
            for lag in range(ROWS):
                h = jnp.broadcast_to(h_ref[pl.ds(lag, 1), c], (nb, LANES))
                for r in range(lag, ROWS):
                    term = h * x[r - lag]
                    y[r] = term if lag == 0 else y[r] + term
            for m in range(modes):
                lam = jnp.broadcast_to(lam_ref[pl.ds(m, 1), c], (nb, LANES))
                q = ps[pl.ds((back * modes + m) * nb, nb), :]
                for r in range(ROWS):
                    q = q * lam
                    y[r] = y[r] + q
            if back:
                y = y[::-1]
            for r in range(ROWS):
                src[pl.ds(r, nb, stride=ROWS), :] = y[r]
        gate_ref[:, c] = grad * xs[...]
        vg_ref[:, c] = us[...].astype(BF16)
        return carry

    lax.fori_loop(0, width // LANES, chunk, 0)


def lane_blocks(rows, width):
    return pl.BlockSpec((rows, width), lambda j: (0, j))


def local_states(v, g, o, lam, d16, width):
    tok, ch = v.shape
    modes = lam.shape[0]
    srows = 2 * modes * (tok // ROWS)
    per = width // LANES * srows
    return pl.pallas_call(
        states_kernel,
        grid=(ch // width,),
        in_specs=[lane_blocks(tok, width)] * 3 + [lane_blocks(modes, width)] * 2,
        out_specs=[pl.BlockSpec((per, LANES), lambda j: (j, 0)), lane_blocks(2 * modes, width)],
        out_shape=[jax.ShapeDtypeStruct((ch // LANES * srows, LANES), F32), jax.ShapeDtypeStruct((2 * modes, ch), F32)],
        scratch_shapes=[pltpu.VMEM((tok, LANES), F32), pltpu.VMEM((tok, LANES), F32)],
        name="states",
    )(v, g, o, lam, d16)


def local_outputs(v, g, o, lam, d16, coef, h, s, incoming, width):
    tok, ch = v.shape
    modes = lam.shape[0]
    srows = 2 * modes * (tok // ROWS)
    per = width // LANES * srows
    return pl.pallas_call(
        outputs_kernel,
        grid=(ch // width,),
        in_specs=[lane_blocks(tok, width)] * 3
        + [lane_blocks(modes, width)] * 3
        + [lane_blocks(ROWS, width), pl.BlockSpec((per, LANES), lambda j: (j, 0)), lane_blocks(2 * modes, width)],
        out_specs=[lane_blocks(tok, width)] * 2,
        out_shape=[jax.ShapeDtypeStruct((tok, ch), F32), jax.ShapeDtypeStruct((tok, ch), BF16)],
        scratch_shapes=[
            pltpu.VMEM((tok, LANES), F32),
            pltpu.VMEM((tok, LANES), F32),
            pltpu.VMEM((srows, LANES), F32),
        ],
        name="outputs",
    )(v, g, o, lam, d16, coef, h, s, incoming)


def swap_cores(a):
    return lax.ppermute(a, "co", [(0, 1), (1, 0)])


def exchange(a, axes):
    return lax.all_to_all(a, axes, split_axis=0, concat_axis=0, tiled=True)


def incoming_states(st, decay, tok):
    _, modes, ch = st.shape
    half = ch // 2
    co = lax.axis_index("co")
    zl = lax.axis_index("zl")
    nz = lax.axis_size("zl")
    other = swap_cores(st)
    first = jnp.where(co == 0, st, other)
    second = jnp.where(co == 0, other, st)
    span = jnp.exp(-decay * tok)

    def mine(a):
        return lax.dynamic_slice_in_dim(a, co * half, half, axis=a.ndim - 1)

    span_h = mine(span)
    first_h, second_h = mine(first), mine(second)
    chip_f = second_h[0] + span_h * first_h[0]
    chip_b = first_h[1] + span_h * second_h[1]
    peers = jnp.arange(nz)
    send = jnp.where((peers > zl)[:, None, None], chip_f[None], chip_b[None])
    got = exchange(send, "zl")
    dist = jnp.abs(peers - zl).astype(F32)
    weight = jnp.exp(-(2.0 * tok) * mine(decay)[None] * jnp.maximum(dist - 1.0, 0.0)[:, None, None])
    got = got * weight
    enter_f = jnp.sum(jnp.where((peers < zl)[:, None, None], got, 0.0), axis=0)
    enter_b = jnp.sum(jnp.where((peers > zl)[:, None, None], got, 0.0), axis=0)
    own = jnp.stack([enter_f, enter_b])
    theirs = swap_cores(own)
    low = jnp.where(co == 0, own, theirs)
    high = jnp.where(co == 0, theirs, own)
    chip_in = jnp.concatenate([low, high], axis=-1)
    in_f = jnp.where(co == 0, chip_in[0], first[0] + span * chip_in[0])
    in_b = jnp.where(co == 1, chip_in[1], second[1] + span * chip_in[1])
    return jnp.concatenate([in_f, in_b], axis=0)


def on_device(inputs, values, gating, out_grad, weight, decay, gain):
    inp, v, g, o = inputs[0], values[0], gating[0], out_grad[0]
    tok, ch = v.shape
    feat = inp.shape[1]
    modes = decay.shape[0]
    nzl, nco, nzh, ny, nx = (lax.axis_size(a) for a in ("zl", "co", "zh", "y", "x"))
    co, zh = lax.axis_index("co"), lax.axis_index("zh")
    blk = weight.shape[0]
    half = ch // nco
    width = min(512, ch)

    lam = jnp.exp(-decay)
    d16 = jnp.exp(-float(ROWS) * decay)
    coef = gain * jnp.sqrt(-jnp.expm1(-2.0 * decay))
    lags = jnp.arange(ROWS, dtype=F32)
    h = jnp.sum(coef[None] * jnp.exp(-decay[None] * lags[:, None, None]), axis=1)

    s, st = local_states(v, g, o, lam, d16, width)
    incoming = incoming_states(st.reshape(2, modes, ch), decay, float(tok))

    in_blocks = inp.reshape(tok, nzh, ny, nx * blk).transpose(2, 0, 1, 3).reshape(ny, tok, -1)
    in_send = jnp.broadcast_to(in_blocks[None], (nco,) + in_blocks.shape).reshape(nco * ny, tok, -1)
    in_rows = exchange(in_send, ("co", "y")).reshape(nco * ny * tok, -1)

    w_half = lax.dynamic_slice_in_dim(weight, co * half, half, axis=1)
    w_x = exchange(jnp.broadcast_to(w_half[None], (nx, blk, half)), "x").reshape(nx * blk, half)
    w_o = lax.ppermute(w_x, "zh", [(0, 1), (1, 0)])
    w_rows = jnp.concatenate([jnp.where(zh == 0, w_x, w_o), jnp.where(zh == 0, w_o, w_x)], axis=0)

    gate_grad, vg = local_outputs(v, g, o, lam, d16, coef, h, s, incoming, width)

    vg_halves = vg.reshape(tok, nco, half).transpose(1, 0, 2)
    vg_send = jnp.broadcast_to(vg_halves[:, None], (nco, ny, tok, half)).reshape(nco * ny, tok, half)
    vg_all = exchange(vg_send, ("co", "y")).reshape(nco * ny * tok, half)

    norm = 1.0 / math.sqrt(tok * nzl * nco * nzh * ny * nx)
    part = norm * lax.dot_general(in_rows, vg_all, (((0,), (0,)), ((), ())), preferred_element_type=F32)
    part = part.astype(BF16).reshape(nzh, nx, blk, half).transpose(1, 0, 2, 3)
    part = jnp.sum(exchange(part, "x").astype(F32), axis=0)
    part = part.reshape(nzh, blk, nzl, half // nzl).transpose(0, 2, 1, 3).reshape(nzh * nzl, blk, half // nzl)
    part = jnp.sum(exchange(part, ("zh", "zl")), axis=0)
    full = exchange(jnp.broadcast_to(part[None], (nzl * nco,) + part.shape), ("zl", "co"))
    weight_grad = full.reshape(nzl, nco, blk, half // nzl).transpose(2, 1, 0, 3).reshape(blk, ch)

    back = lax.dot_general(vg_all, w_rows, (((1,), (1,)), ((), ())), preferred_element_type=F32)
    back = back.astype(BF16).reshape(nco * ny, tok, -1)
    back = jnp.sum(exchange(back, ("co", "y")).astype(F32).reshape(nco, ny, tok, -1), axis=0)
    in_grad = back.reshape(ny, tok, nzh, nx * blk).transpose(1, 2, 0, 3).reshape(tok, feat)
    return (in_grad[None], gate_grad[None], weight_grad)


def solution(mesh):
    n_ctx, n_dp = mesh.devices.shape
    fine = Mesh(mesh.devices.reshape(n_ctx // 2, 2, n_dp // 16, 4, 4), CTX + DP)
    rows = P(DP, CTX, None)
    return jax.shard_map(
        on_device,
        mesh=fine,
        in_specs=(rows, rows, rows, rows, P(DP, None), P(), P()),
        out_specs=(rows, rows, P(DP, None)),
        check_vma=False,
    )
```

```python
import math

import jax
import jax.numpy as jnp
from jax import lax
from jax.experimental import pallas as pl
from jax.experimental.pallas import tpu as pltpu
from jax.sharding import Mesh, PartitionSpec as P

F32 = jnp.float32
BF16 = jnp.bfloat16
LANES = 128
ROWS = 16
RING = 4
CTX = ("zl", "co")
DP = ("zh", "y", "x")


def states_kernel(v_ref, g_ref, o_ref, dec_ref, s_ref, st_ref, xs, us, ls):
    tok, width = v_ref.shape
    modes = dec_ref.shape[0]
    nb = tok // ROWS
    half = modes * nb

    def chunk(j, carry):
        c = pl.ds(pl.multiple_of(j * LANES, LANES), LANES)
        base = pl.multiple_of(j * 2 * half, 2 * half)
        decay = dec_ref[:, c]
        ls[...] = jnp.exp(-decay)
        d16 = jnp.exp(-float(ROWS) * decay)
        xs[...] = v_ref[:, c].astype(F32)
        us[...] = g_ref[:, c].astype(F32) * o_ref[:, c].astype(F32)
        x = [xs[pl.ds(r, nb, stride=ROWS), :] for r in range(ROWS)]
        u = [us[pl.ds(r, nb, stride=ROWS), :] for r in range(ROWS)]
        for m in range(modes):
            lam = jnp.broadcast_to(ls[pl.ds(m, 1), :], (nb, LANES))
            s = x[0]
            b = u[ROWS - 1]
            for r in range(1, ROWS):
                s = s * lam + x[r]
                b = b * lam + u[ROWS - 1 - r]
            s_ref[pl.ds(base + m * nb, nb), :] = s
            s_ref[pl.ds(base + half + m * nb, nb), :] = b
        f = s_ref[pl.ds(base, modes, stride=nb), :]
        b = s_ref[pl.ds(base + half + nb - 1, modes, stride=nb), :]
        for i in range(1, nb):
            f = f * d16 + s_ref[pl.ds(base + i, modes, stride=nb), :]
            b = b * d16 + s_ref[pl.ds(base + half + nb - 1 - i, modes, stride=nb), :]
        st_ref[0:modes, c] = f
        st_ref[modes : 2 * modes, c] = b
        return carry

    lax.fori_loop(0, width // LANES, chunk, 0)


def filter_chunk(src, ps, ls, h_ref, s_ref, in_ref, dec_ref, coef_ref, c, base, back, modes, nb):
    half = modes * nb
    decay = dec_ref[:, c]
    ls[...] = jnp.exp(-decay)
    d16 = jnp.exp(-float(ROWS) * decay)
    coef = coef_ref[:, c]
    p = in_ref[pl.ds(modes if back else 0, modes), c]
    for i in range(nb):
        at = nb - 1 - i if back else i
        ps[pl.ds(at, modes, stride=nb), :] = p * coef
        if i < nb - 1:
            p = p * d16 + s_ref[pl.ds(base + (half if back else 0) + at, modes, stride=nb), :]
    order = list(range(ROWS))
    if back:
        order = order[::-1]
    x = [src[pl.ds(r, nb, stride=ROWS), :] for r in order]
    y = [None] * ROWS
    for lag in range(ROWS):
        h = jnp.broadcast_to(h_ref[pl.ds(lag, 1), c], (nb, LANES))
        for r in range(lag, ROWS):
            term = h * x[r - lag]
            y[r] = term if lag == 0 else y[r] + term
    for m in range(modes):
        lam = jnp.broadcast_to(ls[pl.ds(m, 1), :], (nb, LANES))
        q = ps[pl.ds(m * nb, nb), :]
        for r in range(ROWS):
            q = q * lam
            y[r] = y[r] + q
    for i, r in enumerate(order):
        src[pl.ds(r, nb, stride=ROWS), :] = y[i]


def value_grad_kernel(at_ref, g_ref, o_ref, dec_ref, coef_ref, h_ref, s_ref, in_ref, out_ref, us, ps, ls):
    tok, width = g_ref.shape
    modes = dec_ref.shape[0]
    nb = tok // ROWS

    def chunk(j, carry):
        c = pl.ds(pl.multiple_of(j * LANES, LANES), LANES)
        base = pl.multiple_of(j * 2 * modes * nb, 2 * modes * nb)
        us[...] = g_ref[:, c].astype(F32) * o_ref[:, c].astype(F32)
        filter_chunk(us, ps, ls, h_ref, s_ref, in_ref, dec_ref, coef_ref, c, base, True, modes, nb)
        out_ref[:, c] = us[...].astype(BF16)
        return carry

    lax.fori_loop(0, width // LANES, chunk, 0)


def gate_grad_kernel(v_ref, o_ref, dec_ref, coef_ref, h_ref, s_ref, in_ref, out_ref, xs, ps, ls):
    tok, width = v_ref.shape
    modes = dec_ref.shape[0]
    nb = tok // ROWS

    def chunk(j, carry):
        c = pl.ds(pl.multiple_of(j * LANES, LANES), LANES)
        base = pl.multiple_of(j * 2 * modes * nb, 2 * modes * nb)
        xs[...] = v_ref[:, c].astype(F32)
        filter_chunk(xs, ps, ls, h_ref, s_ref, in_ref, dec_ref, coef_ref, c, base, False, modes, nb)
        out_ref[:, c] = o_ref[:, c].astype(F32) * xs[...]
        return carry

    lax.fori_loop(0, width // LANES, chunk, 0)


def lane_blocks(rows, width):
    return pl.BlockSpec((rows, width), lambda j: (0, j))


def local_states(v, g, o, decay, width):
    tok, ch = v.shape
    modes = decay.shape[0]
    srows = 2 * modes * (tok // ROWS)
    per = width // LANES * srows
    return pl.pallas_call(
        states_kernel,
        grid=(ch // width,),
        in_specs=[lane_blocks(tok, width)] * 3 + [lane_blocks(modes, width)],
        out_specs=[pl.BlockSpec((per, LANES), lambda j: (j, 0)), lane_blocks(2 * modes, width)],
        out_shape=[jax.ShapeDtypeStruct((ch // LANES * srows, LANES), F32), jax.ShapeDtypeStruct((2 * modes, ch), F32)],
        scratch_shapes=[pltpu.VMEM((tok, LANES), F32), pltpu.VMEM((tok, LANES), F32), pltpu.VMEM((modes, LANES), F32)],
        name="states",
    )(v, g, o, decay)


def filter_scratch(tok, modes):
    return [
        pltpu.VMEM((tok, LANES), F32),
        pltpu.VMEM((modes * (tok // ROWS), LANES), F32),
        pltpu.VMEM((modes, LANES), F32),
    ]


def value_grad_half(g, o, decay, coef, h, s, incoming, which, width):
    tok, ch = g.shape
    modes = decay.shape[0]
    per = width // LANES * 2 * modes * (tok // ROWS)
    steps = ch // 2 // width

    def cols(rows):
        return pl.BlockSpec((rows, width), lambda j, at: (0, at[0] * steps + j))

    return pl.pallas_call(
        value_grad_kernel,
        grid_spec=pltpu.PrefetchScalarGridSpec(
            num_scalar_prefetch=1,
            grid=(steps,),
            in_specs=[cols(tok)] * 2
            + [cols(modes)] * 2
            + [cols(ROWS), pl.BlockSpec((per, LANES), lambda j, at: (at[0] * steps + j, 0)), cols(2 * modes)],
            out_specs=pl.BlockSpec((tok, width), lambda j, at: (0, j)),
            scratch_shapes=filter_scratch(tok, modes),
        ),
        out_shape=jax.ShapeDtypeStruct((tok, ch // 2), BF16),
        name="value_grad",
    )(which.reshape(1), g, o, decay, coef, h, s, incoming)


def local_gate_grad(v, o, decay, coef, h, s, incoming, width):
    tok, ch = v.shape
    modes = decay.shape[0]
    per = width // LANES * 2 * modes * (tok // ROWS)
    return pl.pallas_call(
        gate_grad_kernel,
        grid=(ch // width,),
        in_specs=[lane_blocks(tok, width)] * 2
        + [lane_blocks(modes, width)] * 2
        + [lane_blocks(ROWS, width), pl.BlockSpec((per, LANES), lambda j: (j, 0)), lane_blocks(2 * modes, width)],
        out_specs=lane_blocks(tok, width),
        out_shape=jax.ShapeDtypeStruct((tok, ch), F32),
        scratch_shapes=filter_scratch(tok, modes),
        name="gate_grad",
    )(v, o, decay, coef, h, s, incoming)


def smem():
    return pl.BlockSpec(memory_space=pltpu.SMEM)


def vmem():
    return pl.BlockSpec(memory_space=pltpu.VMEM)


def pack_kernel(at_ref, own_ref, other_ref, *refs):
    outs, scr = refs[:RING], refs[RING]
    co, u = at_ref[0], at_ref[1]
    tok, feat = own_ref.shape
    nzh = 2
    strip = feat // (nzh * RING)
    blk = strip // RING
    for k, src in enumerate((own_ref, other_ref)):

        @pl.when(co == 0)
        def _():
            for y in range(RING):
                for zh in range(nzh):
                    scr[y, k, :, zh * strip : (zh + 1) * strip] = src[:, (zh * RING + y) * strip : (zh * RING + y + 1) * strip]

        @pl.when(co == 1)
        def _():
            for x in range(RING):
                for zh in range(nzh):
                    parts = [
                        src[:, (zh * RING + y) * strip + x * blk : (zh * RING + y) * strip + (x + 1) * blk]
                        for y in range(RING)
                    ]
                    scr[x, k, :, zh * strip : (zh + 1) * strip] = jnp.concatenate(parts, axis=1)

    for d in range(RING):
        outs[d][...] = scr[(u + d) % RING]


def pack_inputs(at, own, other):
    tok, feat = own.shape
    piece = (2, tok, feat // RING)
    return pl.pallas_call(
        pack_kernel,
        in_specs=[smem(), vmem(), vmem()],
        out_specs=[vmem()] * RING,
        out_shape=[jax.ShapeDtypeStruct(piece, BF16)] * RING,
        scratch_shapes=[pltpu.VMEM((RING,) + piece, BF16)],
        name="pack_inputs",
    )(at, own, other)


def weight_part_kernel(*refs):
    ins, grads, out, iscr, vscr = refs[:RING], refs[RING : 3 * RING], refs[3 * RING], refs[-2], refs[-1]
    tok = ins[0].shape[1]
    for d in range(RING):
        for k in range(2):
            at = pl.ds((2 * d + k) * tok, tok)
            iscr[at, :] = ins[d][k]
            vscr[at, :] = grads[2 * d + k][...]
    part = lax.dot_general(iscr[...], vscr[...], (((0,), (0,)), ((), ())), preferred_element_type=F32)
    nw, nzh, blk, _ = out.shape
    for zh in range(nzh):
        for w in range(nw):
            at = (zh * nw + w) * blk
            out[w, zh] = part[at : at + blk, :].astype(BF16)


def weight_part(ins, grads):
    _, tok, rows = ins[0].shape
    half = grads[0].shape[1]
    return pl.pallas_call(
        weight_part_kernel,
        in_specs=[vmem()] * (3 * RING),
        out_specs=vmem(),
        out_shape=jax.ShapeDtypeStruct((RING, 2, rows // (2 * RING), half), BF16),
        scratch_shapes=[pltpu.VMEM((2 * RING * tok, rows), BF16), pltpu.VMEM((2 * RING * tok, half), BF16)],
        name="weight_part",
    )(*ins, *grads)


def input_part_kernel(at_ref, *refs):
    ws, grads, outs, wscr, vscr = refs[:RING], refs[RING : 3 * RING], refs[3 * RING : 4 * RING], refs[-2], refs[-1]
    w_at, zh_at = at_ref[2], at_ref[3]
    tok = grads[0].shape[0]
    nzh, blk, _ = ws[0].shape
    for d in range(RING):
        for k in range(nzh):
            zh = (zh_at + k) % nzh
            w = (w_at + RING - d) % RING
            wscr[pl.ds(pl.multiple_of((zh * RING + w) * blk, blk), blk), :] = ws[d][k]
            vscr[pl.ds((2 * d + k) * tok, tok), :] = grads[2 * d + k][...]
    part = lax.dot_general(vscr[...], wscr[...], (((1,), (1,)), ((), ())), preferred_element_type=F32)
    for d in range(RING):
        for k in range(2):
            at = (2 * d + k) * tok
            outs[d][k] = part[at : at + tok, :].astype(BF16)


def input_part(at, ws, grads):
    nzh, blk, half = ws[0].shape
    tok = grads[0].shape[0]
    rows = nzh * RING * blk
    return pl.pallas_call(
        input_part_kernel,
        in_specs=[smem()] + [vmem()] * (3 * RING),
        out_specs=[vmem()] * RING,
        out_shape=[jax.ShapeDtypeStruct((2, tok, rows), BF16)] * RING,
        scratch_shapes=[pltpu.VMEM((rows, half), BF16), pltpu.VMEM((2 * RING * tok, half), BF16)],
        name="input_part",
    )(at, *ws, *grads)


def assemble_kernel(at_ref, *refs):
    own, other, out, scr = refs[:RING], refs[RING], refs[RING + 1], refs[RING + 2]
    co, u, w = at_ref[0], at_ref[1], at_ref[2]
    nzh = 2
    strip = own[0].shape[2] // nzh
    blk = strip // RING
    for d in range(RING):
        scr[co, (u + d) % RING] = own[d][0].astype(F32)
        scr[1 - co, (w + d) % RING] = other[d].astype(F32)
    for zh in range(nzh):
        for y in range(RING):
            rows = scr[0, y, :, zh * strip : (zh + 1) * strip]
            parts = [scr[1, x, :, zh * strip + y * blk : zh * strip + (y + 1) * blk] for x in range(RING)]
            at = (zh * RING + y) * strip
            out[:, at : at + strip] = rows + jnp.concatenate(parts, axis=1)


def assemble(at, own, other):
    _, tok, cols = own[0].shape
    return pl.pallas_call(
        assemble_kernel,
        in_specs=[smem()] + [vmem()] * (RING + 1),
        out_specs=vmem(),
        out_shape=jax.ShapeDtypeStruct((tok, RING * cols), F32),
        scratch_shapes=[pltpu.VMEM((2, RING, tok, cols), F32)],
        name="assemble",
    )(at, *own, other)


RINGS = ("co", "y", "x")


def shift(a, distance, gather):
    pairs = []
    for co in range(2):
        for y in range(RING):
            for x in range(RING):
                if (co == 0) == gather:
                    to = (co, (y + distance) % RING, x)
                else:
                    to = (co, y, (x + distance) % RING)
                pairs.append(((co * RING + y) * RING + x, (to[0] * RING + to[1]) * RING + to[2]))
    return lax.ppermute(a, RINGS, pairs)


def reduce_groups():
    rows = [[(0 * RING + y) * RING + x for x in range(RING)] for y in range(RING)]
    cols = [[(1 * RING + y) * RING + x for y in range(RING)] for x in range(RING)]
    return rows + cols


def swap_cores(a):
    return lax.ppermute(a, "co", [(0, 1), (1, 0)])


def exchange(a, axes, groups=None):
    return lax.all_to_all(a, axes, split_axis=0, concat_axis=0, tiled=True, axis_index_groups=groups)


def incoming_states(st, decay, tok):
    _, modes, ch = st.shape
    half = ch // 2
    co = lax.axis_index("co")
    zl = lax.axis_index("zl")
    nz = lax.axis_size("zl")
    other = swap_cores(st)
    first = jnp.where(co == 0, st, other)
    second = jnp.where(co == 0, other, st)
    span = jnp.exp(-decay * tok)

    def mine(a):
        return lax.dynamic_slice_in_dim(a, co * half, half, axis=a.ndim - 1)

    span_h = mine(span)
    first_h, second_h = mine(first), mine(second)
    chip_f = second_h[0] + span_h * first_h[0]
    chip_b = first_h[1] + span_h * second_h[1]
    peers = jnp.arange(nz)
    send = jnp.where((peers > zl)[:, None, None], chip_f[None], chip_b[None])
    got = exchange(send, "zl")
    dist = jnp.abs(peers - zl).astype(F32)
    weight = jnp.exp(-(2.0 * tok) * mine(decay)[None] * jnp.maximum(dist - 1.0, 0.0)[:, None, None])
    got = got * weight
    enter_f = jnp.sum(jnp.where((peers < zl)[:, None, None], got, 0.0), axis=0)
    enter_b = jnp.sum(jnp.where((peers > zl)[:, None, None], got, 0.0), axis=0)
    own = jnp.stack([enter_f, enter_b])
    theirs = swap_cores(own)
    low = jnp.where(co == 0, own, theirs)
    high = jnp.where(co == 0, theirs, own)
    chip_in = jnp.concatenate([low, high], axis=-1)
    in_f = jnp.where(co == 0, chip_in[0], first[0] + span * chip_in[0])
    in_b = jnp.where(co == 1, chip_in[1], second[1] + span * chip_in[1])
    return jnp.concatenate([in_f, in_b], axis=0)


def on_device(inputs, values, gating, out_grad, weight, decay, gain):
    inp, v, g, o = inputs[0], values[0], gating[0], out_grad[0]
    tok, ch = v.shape
    modes = decay.shape[0]
    nzl, nco, nzh, ny, nx = (lax.axis_size(a) for a in ("zl", "co", "zh", "y", "x"))
    co, zh, y, x = (lax.axis_index(a).astype(jnp.int32) for a in ("co", "zh", "y", "x"))
    gather_at = jnp.where(co == 0, y, x)
    reduce_at = jnp.where(co == 0, x, y)
    at = jnp.stack([co, gather_at, reduce_at, zh])
    blk = weight.shape[0]
    half = ch // nco
    width = min(512, half)

    s, st = local_states(v, g, o, decay, width)

    coef = gain * jnp.sqrt(-jnp.expm1(-2.0 * decay))
    lags = jnp.arange(ROWS, dtype=F32)
    h = jnp.sum(coef[None] * jnp.exp(-decay[None] * lags[:, None, None]), axis=1)

    incoming = incoming_states(st.reshape(2, modes, ch), decay, float(tok))

    packed = pack_inputs(at, inp, swap_cores(inp))
    ins = [packed[0]] + [shift(packed[d], d, True) for d in range(1, RING)]

    w_half = lax.dynamic_slice_in_dim(weight, co * half, half, axis=1)
    w_pair = jnp.stack([w_half, lax.ppermute(w_half, "zh", [(0, 1), (1, 0)])])
    ws = [w_pair] + [shift(w_pair, d, False) for d in range(1, RING)]

    give = value_grad_half(g, o, decay, coef, h, s, incoming, 1 - co, width)
    own = value_grad_half(g, o, decay, coef, h, s, incoming, co, width)
    other = swap_cores(give)
    grads = [own, other]
    for d in range(1, RING):
        grads += [shift(own, d, True), shift(other, d, True)]
    gate_grad = local_gate_grad(v, o, decay, coef, h, s, incoming, width)

    part = exchange(weight_part(ins, grads), RINGS, reduce_groups())
    norm = 1.0 / math.sqrt(tok * nzl * nco * nzh * ny * nx)
    part = norm * jnp.sum(part.astype(F32), axis=0)
    part = part.reshape(nzh, blk, nzl, half // nzl).transpose(0, 2, 1, 3).reshape(nzh * nzl, blk, half // nzl)
    part = jnp.sum(exchange(part, ("zh", "zl")), axis=0)
    full = exchange(jnp.broadcast_to(part[None], (nzl,) + part.shape), "zl")
    full = full.transpose(1, 0, 2).reshape(blk, half)
    rest = swap_cores(full)
    weight_grad = jnp.concatenate([jnp.where(co == 0, full, rest), jnp.where(co == 0, rest, full)], axis=1)

    backs = input_part(at, ws, grads)
    backs = [backs[0]] + [shift(backs[d], -d, True) for d in range(1, RING)]
    theirs = swap_cores(jnp.stack([b[1] for b in backs]))
    in_grad = assemble(at, backs, theirs)
    return (in_grad[None], gate_grad[None], weight_grad)


def solution(mesh):
    n_ctx, n_dp = mesh.devices.shape
    fine = Mesh(mesh.devices.reshape(n_ctx // 2, 2, n_dp // 16, 4, 4), CTX + DP)
    rows = P(DP, CTX, None)
    return jax.shard_map(
        on_device,
        mesh=fine,
        in_specs=(rows, rows, rows, rows, P(DP, None), P(), P()),
        out_specs=(rows, rows, P(DP, None)),
        check_vma=False,
    )
```

```python
import functools
import math

import jax
import jax.numpy as jnp
from jax import lax
from jax.experimental import pallas as pl
from jax.experimental.pallas import tpu as pltpu
from jax.sharding import Mesh, PartitionSpec as P


F32 = jnp.float32
BF16 = jnp.bfloat16
LANES = 128
ROWS = 16
RING = 4
CTX = ("zl", "co")
DP = ("zh", "y", "x")


def far(arrays):
    return [pltpu.with_memory_space_constraint(a, pltpu.HBM) for a in arrays]


def near(arrays):
    return [pltpu.with_memory_space_constraint(a, pltpu.VMEM) for a in arrays]


def params():
    return pltpu.CompilerParams(vmem_limit_bytes=24 * 1024 * 1024)


def states_kernel(v_ref, g_ref, o_ref, dec_ref, s_ref, st_ref, xs, us, ls):
    tok, width = v_ref.shape
    modes = dec_ref.shape[0]
    nb = tok // ROWS
    half = modes * nb

    def chunk(j, carry):
        c = pl.ds(pl.multiple_of(j * LANES, LANES), LANES)
        base = pl.multiple_of(j * 2 * half, 2 * half)
        decay = dec_ref[:, c]
        ls[...] = jnp.exp(-decay)
        d16 = jnp.exp(-float(ROWS) * decay)
        xs[...] = v_ref[:, c].astype(F32)
        us[...] = g_ref[:, c].astype(F32) * o_ref[:, c].astype(F32)
        x = [xs[pl.ds(r, nb, stride=ROWS), :] for r in range(ROWS)]
        u = [us[pl.ds(r, nb, stride=ROWS), :] for r in range(ROWS)]
        for m in range(modes):
            lam = jnp.broadcast_to(ls[pl.ds(m, 1), :], (nb, LANES))
            s = x[0]
            b = u[ROWS - 1]
            for r in range(1, ROWS):
                s = s * lam + x[r]
                b = b * lam + u[ROWS - 1 - r]
            s_ref[pl.ds(base + m * nb, nb), :] = s
            s_ref[pl.ds(base + half + m * nb, nb), :] = b
        f = s_ref[pl.ds(base, modes, stride=nb), :]
        b = s_ref[pl.ds(base + half + nb - 1, modes, stride=nb), :]
        for i in range(1, nb):
            f = f * d16 + s_ref[pl.ds(base + i, modes, stride=nb), :]
            b = b * d16 + s_ref[pl.ds(base + half + nb - 1 - i, modes, stride=nb), :]
        st_ref[0:modes, c] = f
        st_ref[modes : 2 * modes, c] = b
        return carry

    lax.fori_loop(0, width // LANES, chunk, 0)


def filter_chunk(src, ps, ls, h_ref, s_ref, dec_ref, coef_ref, c, base, back, modes, nb, entering):
    decay = dec_ref[:, c]
    ls[...] = jnp.exp(-decay)
    d16 = jnp.exp(-float(ROWS) * decay)
    coef = coef_ref[:, c]
    p = entering
    for i in range(nb):
        at = nb - 1 - i if back else i
        ps[pl.ds(at, modes, stride=nb), :] = p * coef
        if i < nb - 1:
            p = p * d16 + s_ref[pl.ds(base + (modes * nb if back else 0) + at, modes, stride=nb), :]
    order = list(range(ROWS))
    if back:
        order = order[::-1]
    x = [src[pl.ds(r, nb, stride=ROWS), :] for r in order]
    y = [None] * ROWS
    for lag in range(ROWS):
        h = jnp.broadcast_to(h_ref[pl.ds(lag, 1), c], (nb, LANES))
        for r in range(lag, ROWS):
            term = h * x[r - lag]
            y[r] = term if lag == 0 else y[r] + term
    for m in range(modes):
        lam = jnp.broadcast_to(ls[pl.ds(m, 1), :], (nb, LANES))
        q = ps[pl.ds(m * nb, nb), :]
        for r in range(ROWS):
            q = q * lam
            y[r] = y[r] + q
    for i, r in enumerate(order):
        src[pl.ds(r, nb, stride=ROWS), :] = y[i]


def value_grad_kernel(at_ref, g_ref, o_ref, dec_ref, coef_ref, h_ref, s_ref, other_ref, in_ref, out_ref, us, ps, ls):
    tok, width = g_ref.shape
    modes = dec_ref.shape[0]
    nb = tok // ROWS
    co = at_ref[0]

    def chunk(j, carry):
        c = pl.ds(pl.multiple_of(j * LANES, LANES), LANES)
        base = pl.multiple_of(j * 2 * modes * nb, 2 * modes * nb)
        us[...] = g_ref[:, c].astype(F32) * o_ref[:, c].astype(F32)
        chip = in_ref[1, :, c]
        inner = other_ref[modes : 2 * modes, c] + jnp.exp(-float(tok) * dec_ref[:, c]) * chip
        entering = jnp.where(co == 1, chip, inner)
        filter_chunk(us, ps, ls, h_ref, s_ref, dec_ref, coef_ref, c, base, True, modes, nb, entering)
        out_ref[:, c] = us[...].astype(BF16)
        return carry

    lax.fori_loop(0, width // LANES, chunk, 0)


def gate_grad_kernel(
    at_ref, v_ref, o_ref, dec_ref, coef_ref, h_ref, s_ref, other_ref, own_ref, theirs_ref, out_ref, xs, ps, ls
):
    tok, width = v_ref.shape
    modes = dec_ref.shape[0]
    nb = tok // ROWS
    co = at_ref[0]
    own_half = pl.program_id(0) // (pl.num_programs(0) // 2) == co

    def chunk(j, carry):
        c = pl.ds(pl.multiple_of(j * LANES, LANES), LANES)
        base = pl.multiple_of(j * 2 * modes * nb, 2 * modes * nb)
        xs[...] = v_ref[:, c].astype(F32)
        chip = jnp.where(own_half, own_ref[0, :, c], theirs_ref[0, :, c])
        inner = other_ref[0:modes, c] + jnp.exp(-float(tok) * dec_ref[:, c]) * chip
        entering = jnp.where(co == 0, chip, inner)
        filter_chunk(xs, ps, ls, h_ref, s_ref, dec_ref, coef_ref, c, base, False, modes, nb, entering)
        out_ref[:, c] = o_ref[:, c].astype(F32) * xs[...]
        return carry

    lax.fori_loop(0, width // LANES, chunk, 0)


def lane_blocks(rows, width):
    return pl.BlockSpec((rows, width), lambda j: (0, j))


def local_states(v, g, o, decay, width):
    tok, ch = v.shape
    modes = decay.shape[0]
    srows = 2 * modes * (tok // ROWS)
    per = width // LANES * srows
    return pl.pallas_call(
        states_kernel,
        grid=(ch // width,),
        in_specs=[lane_blocks(tok, width)] * 3 + [lane_blocks(modes, width)],
        out_specs=[pl.BlockSpec((per, LANES), lambda j: (j, 0)), lane_blocks(2 * modes, width)],
        out_shape=[pltpu.VMEM((ch // LANES * srows, LANES), F32), pltpu.VMEM((2 * modes, ch), F32)],
        scratch_shapes=[pltpu.VMEM((tok, LANES), F32), pltpu.VMEM((tok, LANES), F32), pltpu.VMEM((modes, LANES), F32)],
        compiler_params=params(),
        name="states",
    )(*far([v, g, o, decay]))


def filter_scratch(tok, modes):
    return [
        pltpu.VMEM((tok, LANES), F32),
        pltpu.VMEM((modes * (tok // ROWS), LANES), F32),
        pltpu.VMEM((modes, LANES), F32),
    ]


def value_grad_half(at, mine, g, o, decay, coef, h, s, other, entry, width):
    tok, ch = g.shape
    modes = decay.shape[0]
    per = width // LANES * 2 * modes * (tok // ROWS)
    steps = ch // 2 // width

    def place(j, at):
        return (at[0] if mine else 1 - at[0]) * steps + j

    def cols(rows):
        return pl.BlockSpec((rows, width), lambda j, at: (0, place(j, at)))

    return pl.pallas_call(
        value_grad_kernel,
        grid_spec=pltpu.PrefetchScalarGridSpec(
            num_scalar_prefetch=1,
            grid=(steps,),
            in_specs=[cols(tok)] * 2
            + [cols(modes)] * 2
            + [
                cols(ROWS),
                pl.BlockSpec((per, LANES), lambda j, at: (place(j, at), 0)),
                cols(2 * modes),
                pl.BlockSpec((2, modes, width), lambda j, at: (0, 0, j)),
            ],
            out_specs=pl.BlockSpec((tok, width), lambda j, at: (0, j)),
            scratch_shapes=filter_scratch(tok, modes),
        ),
        out_shape=jax.ShapeDtypeStruct((tok, ch // 2), BF16),
        compiler_params=params(),
    )(at, *far([g, o, decay]), *near([coef, h]), s, *near([other, entry]))


def local_gate_grad(at, v, o, decay, coef, h, s, other, own, theirs, width):
    tok, ch = v.shape
    modes = decay.shape[0]
    per = width // LANES * 2 * modes * (tok // ROWS)
    steps = ch // 2 // width

    def cols(rows):
        return pl.BlockSpec((rows, width), lambda j, at: (0, j))

    entry = pl.BlockSpec((2, modes, width), lambda j, at: (0, 0, j % steps))
    return pl.pallas_call(
        gate_grad_kernel,
        grid_spec=pltpu.PrefetchScalarGridSpec(
            num_scalar_prefetch=1,
            grid=(2 * steps,),
            in_specs=[cols(tok)] * 2
            + [cols(modes)] * 2
            + [cols(ROWS), pl.BlockSpec((per, LANES), lambda j, at: (j, 0)), cols(2 * modes), entry, entry],
            out_specs=cols(tok),
            scratch_shapes=filter_scratch(tok, modes),
        ),
        out_shape=jax.ShapeDtypeStruct((tok, ch), F32),
        compiler_params=params(),
        name="gate_grad",
    )(at, *far([v, o, decay]), *near([coef, h]), s, *near([other, own, theirs]))


def combine_kernel(at_ref, st_ref, other_ref, dec_ref, *outs, tok):
    co, zl = at_ref[0], at_ref[4]
    modes, half = outs[0].shape
    c = pl.ds(pl.multiple_of(co * half, half), half)
    first = jnp.where(co == 0, st_ref[:, c], other_ref[:, c])
    second = jnp.where(co == 0, other_ref[:, c], st_ref[:, c])
    span = jnp.exp(-tok * dec_ref[:, c])
    chip_f = second[0:modes] + span * first[0:modes]
    chip_b = first[modes:] + span * second[modes:]
    for d in range(1, RING):
        outs[d - 1][...] = jnp.where(zl + d < RING, chip_f, chip_b)


def combine(at, st, other, decay, tok):
    modes, ch = decay.shape
    return pl.pallas_call(
        functools.partial(combine_kernel, tok=tok),
        in_specs=[smem()] + [vmem()] * 3,
        out_specs=[vmem()] * (RING - 1),
        out_shape=[pltpu.VMEM((modes, ch // 2), F32)] * (RING - 1),
        compiler_params=params(),
        name="combine",
    )(at, *near([st, other]), *far([decay]))


def enter_kernel(at_ref, dec_ref, *refs, tok):
    got, out = refs[:-1], refs[-1]
    co, zl = at_ref[0], at_ref[4]
    _, modes, half = out.shape
    decay = dec_ref[:, pl.ds(pl.multiple_of(co * half, half), half)]
    f = jnp.zeros((modes, half), F32)
    b = jnp.zeros((modes, half), F32)
    for d in range(1, RING):
        piece = got[d - 1][...]
        f = f + jnp.where(zl >= d, jnp.exp(-(2.0 * tok * (d - 1)) * decay) * piece, 0.0)
        b = b + jnp.where(zl < d, jnp.exp(-(2.0 * tok * (RING - 1 - d)) * decay) * piece, 0.0)
    out[0] = f
    out[1] = b


def enter(at, decay, got, tok):
    modes, ch = decay.shape
    return pl.pallas_call(
        functools.partial(enter_kernel, tok=tok),
        in_specs=[smem()] + [vmem()] * RING,
        out_specs=vmem(),
        out_shape=pltpu.VMEM((2, modes, ch // 2), F32),
        compiler_params=params(),
        name="enter",
    )(at, *far([decay]), *near(got))


def smem():
    return pl.BlockSpec(memory_space=pltpu.SMEM)


def vmem():
    return pl.BlockSpec(memory_space=pltpu.VMEM)


def pack_kernel(at_ref, own_ref, other_ref, *refs):
    outs, scr = refs[:RING], refs[RING]
    co, u = at_ref[0], at_ref[1]
    _, feat = own_ref.shape
    nzh = 2
    strip = feat // (nzh * RING)
    blk = strip // RING
    for k, src in enumerate((own_ref, other_ref)):

        @pl.when(co == 0)
        def _():
            for y in range(RING):
                for zh in range(nzh):
                    scr[y, k, :, zh * strip : (zh + 1) * strip] = src[:, (zh * RING + y) * strip : (zh * RING + y + 1) * strip]

        @pl.when(co == 1)
        def _():
            for x in range(RING):
                for zh in range(nzh):
                    parts = [
                        src[:, (zh * RING + y) * strip + x * blk : (zh * RING + y) * strip + (x + 1) * blk]
                        for y in range(RING)
                    ]
                    scr[x, k, :, zh * strip : (zh + 1) * strip] = jnp.concatenate(parts, axis=1)

    for d in range(RING):
        outs[d][...] = scr[(u + d) % RING]


def pack_inputs(at, own, other):
    tok, feat = own.shape
    piece = (2, tok, feat // RING)
    return pl.pallas_call(
        pack_kernel,
        in_specs=[smem(), vmem(), vmem()],
        out_specs=[vmem()] * RING,
        out_shape=[pltpu.VMEM(piece, BF16)] * RING,
        scratch_shapes=[pltpu.VMEM((RING,) + piece, BF16)],
        compiler_params=params(),
        name="pack_inputs",
    )(at, *far([own]), *near([other]))


def weight_part_kernel(at_ref, *refs):
    ins, grads = refs[:RING], refs[RING : 3 * RING]
    own, outs, pscr = refs[3 * RING], refs[3 * RING + 1 : 4 * RING], refs[4 * RING]
    w_at = at_ref[2]
    rows = jnp.concatenate([ins[d][k] for d in range(RING) for k in range(2)], axis=0)
    cols = jnp.concatenate([ref[...] for ref in grads], axis=0)
    part = lax.dot_general(rows, cols, (((0,), (0,)), ((), ())), preferred_element_type=F32)
    nzh, blk, _ = own.shape
    for zh in range(nzh):
        for w in range(RING):
            at = (zh * RING + w) * blk
            pscr[w, zh] = part[at : at + blk, :]
    own[...] = pscr[w_at]
    for d in range(1, RING):
        outs[d - 1][...] = pscr[(w_at + d) % RING].astype(BF16)


def weight_part(at, ins, grads):
    _, _, rows = ins[0].shape
    half = grads[0].shape[1]
    piece = (2, rows // (2 * RING), half)
    return pl.pallas_call(
        weight_part_kernel,
        in_specs=[smem()] + [vmem()] * (3 * RING),
        out_specs=[vmem()] * RING,
        out_shape=[pltpu.VMEM(piece, F32)] + [pltpu.VMEM(piece, BF16)] * (RING - 1),
        scratch_shapes=[pltpu.VMEM((RING,) + piece, F32)],
        compiler_params=params(),
        name="weight_part",
    )(at, *near(ins), *near(grads))


def input_part_kernel(at_ref, *refs):
    ws, grads, outs, wscr = refs[:RING], refs[RING : 3 * RING], refs[3 * RING : 4 * RING], refs[4 * RING]
    w_at, zh_at = at_ref[2], at_ref[3]
    tok = grads[0].shape[0]
    nzh, blk, _ = ws[0].shape
    for d in range(RING):
        for k in range(nzh):
            zh = (zh_at + k) % nzh
            w = (w_at + RING - d) % RING
            wscr[pl.ds(pl.multiple_of((zh * RING + w) * blk, blk), blk), :] = ws[d][k]
    rows = jnp.concatenate([ref[...] for ref in grads], axis=0)
    part = lax.dot_general(rows, wscr[...], (((1,), (1,)), ((), ())), preferred_element_type=F32)
    for d in range(RING):
        for k in range(2):
            at = (2 * d + k) * tok
            outs[d][k] = part[at : at + tok, :].astype(BF16)


def input_part(at, ws, grads):
    nzh, blk, half = ws[0].shape
    tok = grads[0].shape[0]
    rows = nzh * RING * blk
    return pl.pallas_call(
        input_part_kernel,
        in_specs=[smem()] + [vmem()] * (3 * RING),
        out_specs=[vmem()] * RING,
        out_shape=[pltpu.VMEM((2, tok, rows), BF16)] * RING,
        scratch_shapes=[pltpu.VMEM((rows, half), BF16)],
        compiler_params=params(),
        name="input_part",
    )(at, *near(ws), *near(grads))


def ring_sum_kernel(at_ref, *refs, norm):
    parts, own, out, scr = refs[:RING], refs[RING], refs[RING + 1], refs[RING + 2]
    total = parts[0][...]
    for d in range(1, RING):
        total = total + parts[d][...].astype(F32)
    total = norm * total
    n, _, quarter = scr.shape
    for zh in range(n // RING):
        for zl in range(RING):
            scr[zh * RING + zl] = total[zh, :, zl * quarter : (zl + 1) * quarter]
    own[...] = scr[at_ref[3] * RING + at_ref[4]]
    out[...] = scr[...].astype(BF16)


def ring_sum(at, parts, norm):
    nzh, blk, half = parts[0].shape
    n = nzh * RING
    piece = (blk, half // RING)
    return pl.pallas_call(
        functools.partial(ring_sum_kernel, norm=norm),
        in_specs=[smem()] + [vmem()] * RING,
        out_specs=[vmem()] * 2,
        out_shape=[pltpu.VMEM(piece, F32), pltpu.VMEM((n,) + piece, BF16)],
        scratch_shapes=[pltpu.VMEM((n,) + piece, F32)],
        compiler_params=params(),
        name="ring_sum",
    )(at, *near(parts))


def line_sum_kernel(at_ref, own_ref, got_ref, out_ref):
    z = at_ref[3] * RING + at_ref[4]
    total = own_ref[...]
    for i in range(got_ref.shape[0]):
        total = total + jnp.where(z == i, 0.0, got_ref[i].astype(F32))
    out_ref[...] = total


def line_sum(at, own, got):
    return pl.pallas_call(
        line_sum_kernel,
        in_specs=[smem()] + [vmem()] * 2,
        out_specs=vmem(),
        out_shape=pltpu.VMEM(own.shape, F32),
        compiler_params=params(),
        name="line_sum",
    )(at, *near([own, got]))


def join_kernel(at_ref, *refs):
    own, theirs, out = refs[:RING], refs[RING : 2 * RING], refs[-1]
    co, zl = at_ref[0], at_ref[4]
    quarter = own[0].shape[1]
    for d in range(RING):
        at = (zl + RING - d) % RING
        out[:, pl.ds(pl.multiple_of((co * RING + at) * quarter, quarter), quarter)] = own[d][...]
        out[:, pl.ds(pl.multiple_of(((1 - co) * RING + at) * quarter, quarter), quarter)] = theirs[d][...]


def join(at, own, theirs):
    blk, quarter = own[0].shape
    return pl.pallas_call(
        join_kernel,
        in_specs=[smem()] + [vmem()] * (2 * RING),
        out_specs=vmem(),
        out_shape=jax.ShapeDtypeStruct((blk, 2 * RING * quarter), F32),
        compiler_params=params(),
        name="join",
    )(at, *near(own), *near(theirs))


def assemble_kernel(at_ref, *refs):
    own, other, out, scr = refs[:RING], refs[RING], refs[RING + 1], refs[RING + 2]
    co, u, w = at_ref[0], at_ref[1], at_ref[2]
    nzh = 2
    strip = own[0].shape[2] // nzh
    blk = strip // RING
    for d in range(RING):
        scr[co, (u + d) % RING] = own[d][0].astype(F32)
        scr[1 - co, (w + d) % RING] = other[d].astype(F32)
    for zh in range(nzh):
        for y in range(RING):
            rows = scr[0, y, :, zh * strip : (zh + 1) * strip]
            parts = [scr[1, x, :, zh * strip + y * blk : zh * strip + (y + 1) * blk] for x in range(RING)]
            at = (zh * RING + y) * strip
            out[:, at : at + strip] = rows + jnp.concatenate(parts, axis=1)


def assemble(at, own, other):
    _, tok, cols = own[0].shape
    return pl.pallas_call(
        assemble_kernel,
        in_specs=[smem()] + [vmem()] * (RING + 1),
        out_specs=vmem(),
        out_shape=jax.ShapeDtypeStruct((tok, RING * cols), F32),
        scratch_shapes=[pltpu.VMEM((2, RING, tok, cols), F32)],
        compiler_params=params(),
        name="assemble",
    )(at, *near(own), *near([other]))


RINGS = ("co", "y", "x")


def shift(a, distance, gather):
    pairs = []
    for co in range(2):
        for y in range(RING):
            for x in range(RING):
                if (co == 0) == gather:
                    to = (co, (y + distance) % RING, x)
                else:
                    to = (co, y, (x + distance) % RING)
                pairs.append(((co * RING + y) * RING + x, (to[0] * RING + to[1]) * RING + to[2]))
    return lax.ppermute(a, RINGS, pairs)


def swap_cores(a):
    return lax.ppermute(a, "co", [(0, 1), (1, 0)])


def along(a, axes, distance):
    n = lax.axis_size(axes)
    return lax.ppermute(a, axes, [(i, (i + distance) % n) for i in range(n)])


def cross(a, distance):
    pairs = []
    for co in range(2):
        for y in range(RING):
            for x in range(RING):
                if co == 1:
                    to = (0, (y + distance) % RING, x)
                else:
                    to = (1, y, (x + distance) % RING)
                pairs.append(((co * RING + y) * RING + x, (to[0] * RING + to[1]) * RING + to[2]))
    return lax.ppermute(a, RINGS, pairs)


def on_device(inputs, values, gating, out_grad, weight, decay, gain):
    return step(inputs[0], values[0], gating[0], out_grad[0], weight, decay, gain)


def step(inp, v, g, o, weight, decay, gain):
    tok, ch = v.shape
    nzl, nco, nzh, ny, nx = (lax.axis_size(a) for a in ("zl", "co", "zh", "y", "x"))
    co, zh, y, x, zl = (lax.axis_index(a).astype(jnp.int32) for a in ("co", "zh", "y", "x", "zl"))
    gather_at = jnp.where(co == 0, y, x)
    reduce_at = jnp.where(co == 0, x, y)
    at = jnp.stack([co, gather_at, reduce_at, zh, zl])
    half = ch // nco
    width = min(512, half)

    w_half = lax.dynamic_slice_in_dim(weight, co * half, half, axis=1)
    w_pair = jnp.stack([w_half, along(w_half, "zh", 1)])
    inp_other = swap_cores(inp)

    s, st = local_states(v, g, o, decay, width)
    other = swap_cores(st)
    coef = gain * jnp.sqrt(-jnp.expm1(-2.0 * decay))
    lags = jnp.arange(ROWS, dtype=F32)
    h = jnp.sum(coef[None] * jnp.exp(-decay[None] * lags[:, None, None]), axis=1)
    send = combine(at, st, other, decay, float(tok))
    ends = []
    for d in range(1, RING):
        ends.append(along(send[d - 1], "zl", d))

    packed = pack_inputs(at, inp, inp_other)
    ins = [packed[0]]
    for d in range(1, RING):
        ins.append(shift(packed[d], d, True))
    ws = [w_pair]
    for d in range(1, RING):
        ws.append(shift(w_pair, d, False))

    own_in = enter(at, decay, ends, float(tok))
    their_in = swap_cores(own_in)
    own = value_grad_half(at, True, g, o, decay, coef, h, s, other, own_in, width)
    give = value_grad_half(at, False, g, o, decay, coef, h, s, other, their_in, width)
    grads = [own, None]
    for d in range(1, RING):
        grads.append(shift(own, d, True))
        grads.append(cross(give, d))
    grads[1] = cross(give, 0)
    gate_grad = local_gate_grad(at, v, o, decay, coef, h, s, other, own_in, their_in, width)

    parts = weight_part(at, ins, grads)
    norm = 1.0 / math.sqrt(tok * nzl * nco * nzh * ny * nx)
    sums = [parts[0]]
    for d in range(1, RING):
        sums.append(shift(parts[d], d, False))
    backs = list(input_part(at, ws, grads))
    for d in range(1, RING):
        backs[d] = shift(backs[d], -d, True)
    pieces = ring_sum(at, sums, norm)
    got = lax.all_to_all(pieces[1], ("zh", "zl"), split_axis=0, concat_axis=0, tiled=True)
    theirs = swap_cores(jnp.stack([b[1] for b in backs]))
    total = line_sum(at, pieces[0], got)
    mine, rest = [total], []
    for d in range(1, nzl):
        mine.append(along(total, "zl", d))
    for d in range(nzl):
        rest.append(swap_cores(mine[d]))
    in_grad = assemble(at, backs, theirs)
    weight_grad = join(at, mine, rest)
    return (in_grad[None], gate_grad[None], weight_grad)


def solution(mesh):
    n_ctx, n_dp = mesh.devices.shape
    fine = Mesh(mesh.devices.reshape(n_ctx // 2, 2, n_dp // 16, 4, 4), CTX + DP)
    rows = P(DP, CTX, None)
    return jax.shard_map(
        on_device,
        mesh=fine,
        in_specs=(rows, rows, rows, rows, P(DP, None), P(), P()),
        out_specs=(rows, rows, P(DP, None)),
        check_vma=False,
    )
```

```python
import functools
import math

import jax
import jax.numpy as jnp
from jax import lax
from jax.experimental import pallas as pl
from jax.experimental.pallas import tpu as pltpu
from jax.sharding import Mesh, PartitionSpec as P


F32 = jnp.float32
BF16 = jnp.bfloat16
LANES = 128
ROWS = 16
RING = 4
CTX = ("zl", "co")
DP = ("zh", "y", "x")


def far(arrays):
    return [pltpu.with_memory_space_constraint(a, pltpu.HBM) for a in arrays]


def near(arrays):
    return [pltpu.with_memory_space_constraint(a, pltpu.VMEM) for a in arrays]


def params():
    return pltpu.CompilerParams(vmem_limit_bytes=24 * 1024 * 1024)


def states_kernel(v_ref, g_ref, o_ref, dec_ref, s_ref, st_ref, xs, us, ls):
    tok, width = v_ref.shape
    modes = dec_ref.shape[0]
    nb = tok // ROWS
    half = modes * nb

    def chunk(j, carry):
        c = pl.ds(pl.multiple_of(j * LANES, LANES), LANES)
        base = pl.multiple_of(j * 2 * half, 2 * half)
        decay = dec_ref[:, c]
        ls[...] = jnp.exp(-decay)
        d16 = jnp.exp(-float(ROWS) * decay)
        xs[...] = v_ref[:, c].astype(F32)
        us[...] = g_ref[:, c].astype(F32) * o_ref[:, c].astype(F32)
        x = [xs[pl.ds(r, nb, stride=ROWS), :] for r in range(ROWS)]
        u = [us[pl.ds(r, nb, stride=ROWS), :] for r in range(ROWS)]
        for m in range(modes):
            lam = jnp.broadcast_to(ls[pl.ds(m, 1), :], (nb, LANES))
            s = x[0]
            b = u[ROWS - 1]
            for r in range(1, ROWS):
                s = s * lam + x[r]
                b = b * lam + u[ROWS - 1 - r]
            s_ref[pl.ds(base + m * nb, nb), :] = s
            s_ref[pl.ds(base + half + m * nb, nb), :] = b
        f = s_ref[pl.ds(base, modes, stride=nb), :]
        b = s_ref[pl.ds(base + half + nb - 1, modes, stride=nb), :]
        for i in range(1, nb):
            f = f * d16 + s_ref[pl.ds(base + i, modes, stride=nb), :]
            b = b * d16 + s_ref[pl.ds(base + half + nb - 1 - i, modes, stride=nb), :]
        st_ref[0:modes, c] = f
        st_ref[modes : 2 * modes, c] = b
        return carry

    lax.fori_loop(0, width // LANES, chunk, 0)


def filter_chunk(src, ps, ls, h_ref, s_ref, dec_ref, coef_ref, c, base, back, modes, nb, entering):
    decay = dec_ref[:, c]
    ls[...] = jnp.exp(-decay)
    d16 = jnp.exp(-float(ROWS) * decay)
    coef = coef_ref[:, c]
    p = entering
    for i in range(nb):
        at = nb - 1 - i if back else i
        ps[pl.ds(at, modes, stride=nb), :] = p * coef
        if i < nb - 1:
            p = p * d16 + s_ref[pl.ds(base + (modes * nb if back else 0) + at, modes, stride=nb), :]
    order = list(range(ROWS))
    if back:
        order = order[::-1]
    x = [src[pl.ds(r, nb, stride=ROWS), :] for r in order]
    y = [None] * ROWS
    for lag in range(ROWS):
        h = jnp.broadcast_to(h_ref[pl.ds(lag, 1), c], (nb, LANES))
        for r in range(lag, ROWS):
            term = h * x[r - lag]
            y[r] = term if lag == 0 else y[r] + term
    for m in range(modes):
        lam = jnp.broadcast_to(ls[pl.ds(m, 1), :], (nb, LANES))
        q = ps[pl.ds(m * nb, nb), :]
        for r in range(ROWS):
            q = q * lam
            y[r] = y[r] + q
    for i, r in enumerate(order):
        src[pl.ds(r, nb, stride=ROWS), :] = y[i]


def value_grad_kernel(at_ref, g_ref, o_ref, dec_ref, coef_ref, h_ref, s_ref, other_ref, in_ref, out_ref, us, ps, ls):
    tok, width = g_ref.shape
    modes = dec_ref.shape[0]
    nb = tok // ROWS
    co = at_ref[0]

    def chunk(j, carry):
        c = pl.ds(pl.multiple_of(j * LANES, LANES), LANES)
        base = pl.multiple_of(j * 2 * modes * nb, 2 * modes * nb)
        us[...] = g_ref[:, c].astype(F32) * o_ref[:, c].astype(F32)
        chip = in_ref[1, :, c]
        inner = other_ref[modes : 2 * modes, c] + jnp.exp(-float(tok) * dec_ref[:, c]) * chip
        entering = jnp.where(co == 1, chip, inner)
        filter_chunk(us, ps, ls, h_ref, s_ref, dec_ref, coef_ref, c, base, True, modes, nb, entering)
        out_ref[:, c] = us[...].astype(BF16)
        return carry

    lax.fori_loop(0, width // LANES, chunk, 0)


def gate_grad_kernel(
    at_ref, v_ref, o_ref, dec_ref, coef_ref, h_ref, s_ref, other_ref, own_ref, theirs_ref, out_ref, xs, ps, ls
):
    tok, width = v_ref.shape
    modes = dec_ref.shape[0]
    nb = tok // ROWS
    co = at_ref[0]
    own_half = pl.program_id(0) // (pl.num_programs(0) // 2) == co

    def chunk(j, carry):
        c = pl.ds(pl.multiple_of(j * LANES, LANES), LANES)
        base = pl.multiple_of(j * 2 * modes * nb, 2 * modes * nb)
        xs[...] = v_ref[:, c].astype(F32)
        chip = jnp.where(own_half, own_ref[0, :, c], theirs_ref[0, :, c])
        inner = other_ref[0:modes, c] + jnp.exp(-float(tok) * dec_ref[:, c]) * chip
        entering = jnp.where(co == 0, chip, inner)
        filter_chunk(xs, ps, ls, h_ref, s_ref, dec_ref, coef_ref, c, base, False, modes, nb, entering)
        out_ref[:, c] = o_ref[:, c].astype(F32) * xs[...]
        return carry

    lax.fori_loop(0, width // LANES, chunk, 0)


def lane_blocks(rows, width):
    return pl.BlockSpec((rows, width), lambda j: (0, j))


def local_states(v, g, o, decay, width):
    tok, ch = v.shape
    modes = decay.shape[0]
    srows = 2 * modes * (tok // ROWS)
    per = width // LANES * srows
    return pl.pallas_call(
        states_kernel,
        grid=(ch // width,),
        in_specs=[lane_blocks(tok, width)] * 3 + [lane_blocks(modes, width)],
        out_specs=[pl.BlockSpec((per, LANES), lambda j: (j, 0)), lane_blocks(2 * modes, width)],
        out_shape=[pltpu.VMEM((ch // LANES * srows, LANES), F32), pltpu.VMEM((2 * modes, ch), F32)],
        scratch_shapes=[pltpu.VMEM((tok, LANES), F32), pltpu.VMEM((tok, LANES), F32), pltpu.VMEM((modes, LANES), F32)],
        compiler_params=params(),
        name="states",
    )(*far([v, g, o, decay]))


def filter_scratch(tok, modes):
    return [
        pltpu.VMEM((tok, LANES), F32),
        pltpu.VMEM((modes * (tok // ROWS), LANES), F32),
        pltpu.VMEM((modes, LANES), F32),
    ]


def value_grad_half(at, mine, g, o, decay, coef, h, s, other, entry, width):
    tok, ch = g.shape
    modes = decay.shape[0]
    per = width // LANES * 2 * modes * (tok // ROWS)
    steps = ch // 2 // width

    def place(j, at):
        return (at[0] if mine else 1 - at[0]) * steps + j

    def cols(rows):
        return pl.BlockSpec((rows, width), lambda j, at: (0, place(j, at)))

    return pl.pallas_call(
        value_grad_kernel,
        grid_spec=pltpu.PrefetchScalarGridSpec(
            num_scalar_prefetch=1,
            grid=(steps,),
            in_specs=[cols(tok)] * 2
            + [cols(modes)] * 2
            + [
                cols(ROWS),
                pl.BlockSpec((per, LANES), lambda j, at: (place(j, at), 0)),
                cols(2 * modes),
                pl.BlockSpec((2, modes, width), lambda j, at: (0, 0, j)),
            ],
            out_specs=pl.BlockSpec((tok, width), lambda j, at: (0, j)),
            scratch_shapes=filter_scratch(tok, modes),
        ),
        out_shape=jax.ShapeDtypeStruct((tok, ch // 2), BF16),
        compiler_params=params(),
    )(at, *far([g, o, decay]), *near([coef, h]), s, *near([other, entry]))


def local_gate_grad(at, v, o, decay, coef, h, s, other, own, theirs, width):
    tok, ch = v.shape
    modes = decay.shape[0]
    per = width // LANES * 2 * modes * (tok // ROWS)
    steps = ch // 2 // width

    def cols(rows):
        return pl.BlockSpec((rows, width), lambda j, at: (0, j))

    entry = pl.BlockSpec((2, modes, width), lambda j, at: (0, 0, j % steps))
    return pl.pallas_call(
        gate_grad_kernel,
        grid_spec=pltpu.PrefetchScalarGridSpec(
            num_scalar_prefetch=1,
            grid=(2 * steps,),
            in_specs=[cols(tok)] * 2
            + [cols(modes)] * 2
            + [cols(ROWS), pl.BlockSpec((per, LANES), lambda j, at: (j, 0)), cols(2 * modes), entry, entry],
            out_specs=cols(tok),
            scratch_shapes=filter_scratch(tok, modes),
        ),
        out_shape=jax.ShapeDtypeStruct((tok, ch), F32),
        compiler_params=params(),
        name="gate_grad",
    )(at, *far([v, o, decay]), *near([coef, h]), s, *near([other]), *far([own, theirs]))


def combine_kernel(at_ref, st_ref, other_ref, dec_ref, *outs, tok):
    co, zl = at_ref[0], at_ref[4]
    modes, half = outs[0].shape
    c = pl.ds(pl.multiple_of(co * half, half), half)
    first = jnp.where(co == 0, st_ref[:, c], other_ref[:, c])
    second = jnp.where(co == 0, other_ref[:, c], st_ref[:, c])
    span = jnp.exp(-tok * dec_ref[:, c])
    chip_f = second[0:modes] + span * first[0:modes]
    chip_b = first[modes:] + span * second[modes:]
    for d in range(1, RING):
        outs[d - 1][...] = jnp.where(zl + d < RING, chip_f, chip_b)


def combine(at, st, other, decay, tok):
    modes, ch = decay.shape
    return pl.pallas_call(
        functools.partial(combine_kernel, tok=tok),
        in_specs=[smem()] + [vmem()] * 3,
        out_specs=[vmem()] * (RING - 1),
        out_shape=[pltpu.VMEM((modes, ch // 2), F32)] * (RING - 1),
        compiler_params=params(),
        name="combine",
    )(at, *near([st, other]), *far([decay]))


def enter_kernel(at_ref, dec_ref, *refs, tok):
    got, out = refs[:-1], refs[-1]
    co, zl = at_ref[0], at_ref[4]
    _, modes, half = out.shape
    decay = dec_ref[:, pl.ds(pl.multiple_of(co * half, half), half)]
    f = jnp.zeros((modes, half), F32)
    b = jnp.zeros((modes, half), F32)
    for d in range(1, RING):
        piece = got[d - 1][...]
        f = f + jnp.where(zl >= d, jnp.exp(-(2.0 * tok * (d - 1)) * decay) * piece, 0.0)
        b = b + jnp.where(zl < d, jnp.exp(-(2.0 * tok * (RING - 1 - d)) * decay) * piece, 0.0)
    out[0] = f
    out[1] = b


def enter(at, decay, got, tok):
    modes, ch = decay.shape
    return pl.pallas_call(
        functools.partial(enter_kernel, tok=tok),
        in_specs=[smem()] + [vmem()] * RING,
        out_specs=vmem(),
        out_shape=pltpu.VMEM((2, modes, ch // 2), F32),
        compiler_params=params(),
        name="enter",
    )(at, *far([decay]), *near(got))


def smem():
    return pl.BlockSpec(memory_space=pltpu.SMEM)


def vmem():
    return pl.BlockSpec(memory_space=pltpu.VMEM)


def pack_kernel(at_ref, own_ref, other_ref, *refs):
    outs, scr = refs[:RING], refs[RING]
    co, u = at_ref[0], at_ref[1]
    _, feat = own_ref.shape
    nzh = 2
    strip = feat // (nzh * RING)
    blk = strip // RING
    for k, src in enumerate((own_ref, other_ref)):

        @pl.when(co == 0)
        def _():
            for y in range(RING):
                for zh in range(nzh):
                    scr[y, k, :, zh * strip : (zh + 1) * strip] = src[:, (zh * RING + y) * strip : (zh * RING + y + 1) * strip]

        @pl.when(co == 1)
        def _():
            for x in range(RING):
                for zh in range(nzh):
                    parts = [
                        src[:, (zh * RING + y) * strip + x * blk : (zh * RING + y) * strip + (x + 1) * blk]
                        for y in range(RING)
                    ]
                    scr[x, k, :, zh * strip : (zh + 1) * strip] = jnp.concatenate(parts, axis=1)

    for d in range(RING):
        outs[d][...] = scr[(u + d) % RING]


def pack_inputs(at, own, other):
    tok, feat = own.shape
    piece = (2, tok, feat // RING)
    return pl.pallas_call(
        pack_kernel,
        in_specs=[smem(), vmem(), vmem()],
        out_specs=[vmem()] * RING,
        out_shape=[pltpu.VMEM(piece, BF16)] * RING,
        scratch_shapes=[pltpu.VMEM((RING,) + piece, BF16)],
        compiler_params=params(),
        name="pack_inputs",
    )(at, *far([own]), *near([other]))


def weight_part_kernel(at_ref, *refs):
    ins, grads = refs[:RING], refs[RING : 3 * RING]
    own, outs, pscr = refs[3 * RING], refs[3 * RING + 1 : 4 * RING], refs[4 * RING]
    w_at = at_ref[2]
    rows = jnp.concatenate([ins[d][k] for d in range(RING) for k in range(2)], axis=0)
    cols = jnp.concatenate([ref[...] for ref in grads], axis=0)
    part = lax.dot_general(rows, cols, (((0,), (0,)), ((), ())), preferred_element_type=F32)
    nzh, blk, _ = own.shape
    for zh in range(nzh):
        for w in range(RING):
            at = (zh * RING + w) * blk
            pscr[w, zh] = part[at : at + blk, :]
    own[...] = pscr[w_at]
    for d in range(1, RING):
        outs[d - 1][...] = pscr[(w_at + d) % RING].astype(BF16)


def weight_part(at, ins, grads):
    _, _, rows = ins[0].shape
    half = grads[0].shape[1]
    piece = (2, rows // (2 * RING), half)
    return pl.pallas_call(
        weight_part_kernel,
        in_specs=[smem()] + [vmem()] * (3 * RING),
        out_specs=[vmem()] * RING,
        out_shape=[pltpu.VMEM(piece, F32)] + [pltpu.VMEM(piece, BF16)] * (RING - 1),
        scratch_shapes=[pltpu.VMEM((RING,) + piece, F32)],
        compiler_params=params(),
        name="weight_part",
    )(at, *near(ins), *near(grads))


def input_part_kernel(at_ref, *refs):
    ws, grads, outs, wscr = refs[:RING], refs[RING : 3 * RING], refs[3 * RING : 4 * RING], refs[4 * RING]
    w_at, zh_at = at_ref[2], at_ref[3]
    tok = grads[0].shape[0]
    nzh, blk, _ = ws[0].shape
    for d in range(RING):
        for k in range(nzh):
            zh = (zh_at + k) % nzh
            w = (w_at + RING - d) % RING
            wscr[pl.ds(pl.multiple_of((zh * RING + w) * blk, blk), blk), :] = ws[d][k]
    rows = jnp.concatenate([ref[...] for ref in grads], axis=0)
    part = lax.dot_general(rows, wscr[...], (((1,), (1,)), ((), ())), preferred_element_type=F32)
    for d in range(RING):
        for k in range(2):
            at = (2 * d + k) * tok
            outs[d][k] = part[at : at + tok, :].astype(BF16)


def input_part(at, ws, grads):
    nzh, blk, half = ws[0].shape
    tok = grads[0].shape[0]
    rows = nzh * RING * blk
    return pl.pallas_call(
        input_part_kernel,
        in_specs=[smem()] + [vmem()] * (3 * RING),
        out_specs=[vmem()] * RING,
        out_shape=[pltpu.VMEM((2, tok, rows), BF16)] * RING,
        scratch_shapes=[pltpu.VMEM((rows, half), BF16)],
        compiler_params=params(),
        name="input_part",
    )(at, *near(ws), *far(grads))


def stack_kernel(*refs):
    for i, ref in enumerate(refs[:-1]):
        refs[-1][i] = ref[...]


def stack(parts):
    return pl.pallas_call(
        stack_kernel,
        in_specs=[vmem()] * len(parts),
        out_specs=vmem(),
        out_shape=pltpu.VMEM((len(parts),) + parts[0].shape, parts[0].dtype),
        compiler_params=params(),
        name="stack",
    )(*near(parts))


def pick_kernel(*refs):
    for i, ref in enumerate(refs[:-1]):
        refs[-1][i] = ref[1]


def pick_other(parts):
    return pl.pallas_call(
        pick_kernel,
        in_specs=[vmem()] * len(parts),
        out_specs=vmem(),
        out_shape=pltpu.VMEM((len(parts),) + parts[0].shape[1:], parts[0].dtype),
        compiler_params=params(),
        name="pick_other",
    )(*near(parts))


def ring_sum_kernel(at_ref, *refs, norm):
    parts, own, out, scr = refs[:RING], refs[RING], refs[RING + 1], refs[RING + 2]
    total = parts[0][...]
    for d in range(1, RING):
        total = total + parts[d][...].astype(F32)
    total = norm * total
    n, _, quarter = scr.shape
    for zh in range(n // RING):
        for zl in range(RING):
            scr[zh * RING + zl] = total[zh, :, zl * quarter : (zl + 1) * quarter]
    own[...] = scr[at_ref[3] * RING + at_ref[4]]
    out[...] = scr[...].astype(BF16)


def ring_sum(at, parts, norm):
    nzh, blk, half = parts[0].shape
    n = nzh * RING
    piece = (blk, half // RING)
    return pl.pallas_call(
        functools.partial(ring_sum_kernel, norm=norm),
        in_specs=[smem()] + [vmem()] * RING,
        out_specs=[vmem()] * 2,
        out_shape=[pltpu.VMEM(piece, F32), pltpu.VMEM((n,) + piece, BF16)],
        scratch_shapes=[pltpu.VMEM((n,) + piece, F32)],
        compiler_params=params(),
        name="ring_sum",
    )(at, *near(parts))


def line_sum_kernel(at_ref, own_ref, got_ref, out_ref):
    z = at_ref[3] * RING + at_ref[4]
    total = own_ref[...]
    for i in range(got_ref.shape[0]):
        total = total + jnp.where(z == i, 0.0, got_ref[i].astype(F32))
    out_ref[...] = total


def line_sum(at, own, got):
    return pl.pallas_call(
        line_sum_kernel,
        in_specs=[smem()] + [vmem()] * 2,
        out_specs=vmem(),
        out_shape=pltpu.VMEM(own.shape, F32),
        compiler_params=params(),
        name="line_sum",
    )(at, *near([own, got]))


def join_kernel(at_ref, *refs):
    own, theirs, out = refs[:RING], refs[RING : 2 * RING], refs[-1]
    co, zl = at_ref[0], at_ref[4]
    quarter = own[0].shape[1]
    for d in range(RING):
        at = (zl + RING - d) % RING
        out[:, pl.ds(pl.multiple_of((co * RING + at) * quarter, quarter), quarter)] = own[d][...]
        out[:, pl.ds(pl.multiple_of(((1 - co) * RING + at) * quarter, quarter), quarter)] = theirs[d][...]


def join(at, own, theirs):
    blk, quarter = own[0].shape
    return pl.pallas_call(
        join_kernel,
        in_specs=[smem()] + [vmem()] * (2 * RING),
        out_specs=vmem(),
        out_shape=jax.ShapeDtypeStruct((blk, 2 * RING * quarter), F32),
        compiler_params=params(),
        name="join",
    )(at, *near(own), *near(theirs))


def assemble_kernel(at_ref, *refs):
    own, other, out, scr = refs[:RING], refs[RING], refs[RING + 1], refs[RING + 2]
    co, u, w = at_ref[0], at_ref[1], at_ref[2]
    nzh = 2
    strip = own[0].shape[2] // nzh
    blk = strip // RING
    for d in range(RING):
        scr[co, (u + d) % RING] = own[d][0].astype(F32)
        scr[1 - co, (w + d) % RING] = other[d].astype(F32)
    for zh in range(nzh):
        for y in range(RING):
            rows = scr[0, y, :, zh * strip : (zh + 1) * strip]
            parts = [scr[1, x, :, zh * strip + y * blk : zh * strip + (y + 1) * blk] for x in range(RING)]
            at = (zh * RING + y) * strip
            out[:, at : at + strip] = rows + jnp.concatenate(parts, axis=1)


def assemble(at, own, other):
    _, tok, cols = own[0].shape
    return pl.pallas_call(
        assemble_kernel,
        in_specs=[smem()] + [vmem()] * (RING + 1),
        out_specs=vmem(),
        out_shape=jax.ShapeDtypeStruct((tok, RING * cols), F32),
        scratch_shapes=[pltpu.VMEM((2, RING, tok, cols), F32)],
        compiler_params=params(),
        name="assemble",
    )(at, *near(own), *near([other]))


RINGS = ("co", "y", "x")


def shift(a, distance, gather):
    pairs = []
    for co in range(2):
        for y in range(RING):
            for x in range(RING):
                if (co == 0) == gather:
                    to = (co, (y + distance) % RING, x)
                else:
                    to = (co, y, (x + distance) % RING)
                pairs.append(((co * RING + y) * RING + x, (to[0] * RING + to[1]) * RING + to[2]))
    return lax.ppermute(a, RINGS, pairs)


def swap_cores(a):
    return lax.ppermute(a, "co", [(0, 1), (1, 0)])


def along(a, axes, distance):
    n = lax.axis_size(axes)
    return lax.ppermute(a, axes, [(i, (i + distance) % n) for i in range(n)])


def cross(a, distance):
    pairs = []
    for co in range(2):
        for y in range(RING):
            for x in range(RING):
                if co == 1:
                    to = (0, (y + distance) % RING, x)
                else:
                    to = (1, y, (x + distance) % RING)
                pairs.append(((co * RING + y) * RING + x, (to[0] * RING + to[1]) * RING + to[2]))
    return lax.ppermute(a, RINGS, pairs)


def on_device(inputs, values, gating, out_grad, weight, decay, gain):
    return step(inputs[0], values[0], gating[0], out_grad[0], weight, decay, gain)


def step(inp, v, g, o, weight, decay, gain):
    tok, ch = v.shape
    nzl, nco, nzh, ny, nx = (lax.axis_size(a) for a in ("zl", "co", "zh", "y", "x"))
    co, zh, y, x, zl = (lax.axis_index(a).astype(jnp.int32) for a in ("co", "zh", "y", "x", "zl"))
    gather_at = jnp.where(co == 0, y, x)
    reduce_at = jnp.where(co == 0, x, y)
    at = jnp.stack([co, gather_at, reduce_at, zh, zl])
    half = ch // nco
    width = min(512, half)

    w_half = lax.dynamic_slice_in_dim(weight, co * half, half, axis=1)
    w_other = along(w_half, "zh", 1)
    w_pair = stack([w_half, w_other])
    inp_other = swap_cores(inp)

    s, st = local_states(v, g, o, decay, width)
    other = swap_cores(st)
    coef = gain * jnp.sqrt(-jnp.expm1(-2.0 * decay))
    lags = jnp.arange(ROWS, dtype=F32)
    h = jnp.sum(coef[None] * jnp.exp(-decay[None] * lags[:, None, None]), axis=1)
    send = combine(at, st, other, decay, float(tok))
    ends = []
    for d in range(1, RING):
        ends.append(along(send[d - 1], "zl", d))

    packed = pack_inputs(at, inp, inp_other)
    ins = [packed[0]]
    for d in range(1, RING):
        ins.append(shift(packed[d], d, True))
    ws = [w_pair]
    for d in range(1, RING):
        ws.append(shift(w_pair, d, False))

    own_in = enter(at, decay, ends, float(tok))
    their_in = swap_cores(own_in)
    own = value_grad_half(at, True, g, o, decay, coef, h, s, other, own_in, width)
    give = value_grad_half(at, False, g, o, decay, coef, h, s, other, their_in, width)
    grads = [own, None]
    for d in range(1, RING):
        grads.append(shift(own, d, True))
        grads.append(cross(give, d))
    grads[1] = cross(give, 0)
    gate_grad = local_gate_grad(at, v, o, decay, coef, h, s, other, own_in, their_in, width)

    parts = weight_part(at, ins, grads)
    norm = 1.0 / math.sqrt(tok * nzl * nco * nzh * ny * nx)
    sums = [parts[0]]
    for d in range(1, RING):
        sums.append(shift(parts[d], d, False))
    backs = list(input_part(at, ws, grads))
    for d in range(1, RING):
        backs[d] = shift(backs[d], -d, True)
    pieces = ring_sum(at, sums, norm)
    got = lax.all_to_all(pieces[1], ("zh", "zl"), split_axis=0, concat_axis=0, tiled=True)
    picked = pick_other(backs)
    theirs = swap_cores(picked)
    total = line_sum(at, pieces[0], got)
    mine, rest = [total], []
    for d in range(1, nzl):
        mine.append(along(total, "zl", d))
    for d in range(nzl):
        rest.append(swap_cores(mine[d]))
    in_grad = assemble(at, backs, theirs)
    weight_grad = join(at, mine, rest)
    return (in_grad[None], gate_grad[None], weight_grad)


def solution(mesh):
    n_ctx, n_dp = mesh.devices.shape
    fine = Mesh(mesh.devices.reshape(n_ctx // 2, 2, n_dp // 16, 4, 4), CTX + DP)
    rows = P(DP, CTX, None)
    return jax.shard_map(
        on_device,
        mesh=fine,
        in_specs=(rows, rows, rows, rows, P(DP, None), P(), P()),
        out_specs=(rows, rows, P(DP, None)),
        check_vma=False,
    )
```

```python
import functools
import math

import jax
import jax.numpy as jnp
from jax import lax
from jax.experimental import pallas as pl
from jax.experimental.pallas import tpu as pltpu
from jax.sharding import Mesh, PartitionSpec as P


F32 = jnp.float32
BF16 = jnp.bfloat16
LANES = 128
ROWS = 16
RING = 4
CTX = ("zl", "co")
DP = ("zh", "y", "x")


def far(arrays):
    return [pltpu.with_memory_space_constraint(a, pltpu.HBM) for a in arrays]


def near(arrays):
    return [pltpu.with_memory_space_constraint(a, pltpu.VMEM) for a in arrays]


def params():
    return pltpu.CompilerParams(vmem_limit_bytes=24 * 1024 * 1024)


def states_kernel(v_ref, g_ref, o_ref, dec_ref, s_ref, st_ref, xs, us, ls):
    tok, width = v_ref.shape
    modes = dec_ref.shape[0]
    nb = tok // ROWS
    half = modes * nb

    def chunk(j, carry):
        c = pl.ds(pl.multiple_of(j * LANES, LANES), LANES)
        base = pl.multiple_of(j * 2 * half, 2 * half)
        decay = dec_ref[:, c]
        ls[...] = jnp.exp(-decay)
        d16 = jnp.exp(-float(ROWS) * decay)
        xs[...] = v_ref[:, c].astype(F32)
        us[...] = g_ref[:, c].astype(F32) * o_ref[:, c].astype(F32)
        x = [xs[pl.ds(r, nb, stride=ROWS), :] for r in range(ROWS)]
        u = [us[pl.ds(r, nb, stride=ROWS), :] for r in range(ROWS)]
        for m in range(modes):
            lam = jnp.broadcast_to(ls[pl.ds(m, 1), :], (nb, LANES))
            s = x[0]
            b = u[ROWS - 1]
            for r in range(1, ROWS):
                s = s * lam + x[r]
                b = b * lam + u[ROWS - 1 - r]
            s_ref[pl.ds(base + m * nb, nb), :] = s
            s_ref[pl.ds(base + half + m * nb, nb), :] = b
        f = s_ref[pl.ds(base, modes, stride=nb), :]
        b = s_ref[pl.ds(base + half + nb - 1, modes, stride=nb), :]
        for i in range(1, nb):
            f = f * d16 + s_ref[pl.ds(base + i, modes, stride=nb), :]
            b = b * d16 + s_ref[pl.ds(base + half + nb - 1 - i, modes, stride=nb), :]
        st_ref[0:modes, c] = f
        st_ref[modes : 2 * modes, c] = b
        return carry

    lax.fori_loop(0, width // LANES, chunk, 0)


def filter_chunk(src, ps, ls, h_ref, s_ref, dec_ref, coef_ref, c, base, back, modes, nb, entering):
    decay = dec_ref[:, c]
    ls[...] = jnp.exp(-decay)
    d16 = jnp.exp(-float(ROWS) * decay)
    coef = coef_ref[:, c]
    p = entering
    for i in range(nb):
        at = nb - 1 - i if back else i
        ps[pl.ds(at, modes, stride=nb), :] = p * coef
        if i < nb - 1:
            p = p * d16 + s_ref[pl.ds(base + (modes * nb if back else 0) + at, modes, stride=nb), :]
    order = list(range(ROWS))
    if back:
        order = order[::-1]
    x = [src[pl.ds(r, nb, stride=ROWS), :] for r in order]
    y = [None] * ROWS
    for lag in range(ROWS):
        h = jnp.broadcast_to(h_ref[pl.ds(lag, 1), c], (nb, LANES))
        for r in range(lag, ROWS):
            term = h * x[r - lag]
            y[r] = term if lag == 0 else y[r] + term
    for m in range(modes):
        lam = jnp.broadcast_to(ls[pl.ds(m, 1), :], (nb, LANES))
        q = ps[pl.ds(m * nb, nb), :]
        for r in range(ROWS):
            q = q * lam
            y[r] = y[r] + q
    for i, r in enumerate(order):
        src[pl.ds(r, nb, stride=ROWS), :] = y[i]


def value_grad_kernel(at_ref, g_ref, o_ref, dec_ref, coef_ref, h_ref, s_ref, other_ref, in_ref, out_ref, us, ps, ls):
    tok, width = g_ref.shape
    modes = dec_ref.shape[0]
    nb = tok // ROWS
    co = at_ref[0]

    def chunk(j, carry):
        c = pl.ds(pl.multiple_of(j * LANES, LANES), LANES)
        base = pl.multiple_of(j * 2 * modes * nb, 2 * modes * nb)
        us[...] = g_ref[:, c].astype(F32) * o_ref[:, c].astype(F32)
        chip = in_ref[1, :, c]
        inner = other_ref[modes : 2 * modes, c] + jnp.exp(-float(tok) * dec_ref[:, c]) * chip
        entering = jnp.where(co == 1, chip, inner)
        filter_chunk(us, ps, ls, h_ref, s_ref, dec_ref, coef_ref, c, base, True, modes, nb, entering)
        out_ref[:, c] = us[...].astype(BF16)
        return carry

    lax.fori_loop(0, width // LANES, chunk, 0)


def gate_grad_kernel(
    at_ref, v_ref, o_ref, dec_ref, coef_ref, h_ref, s_ref, other_ref, own_ref, theirs_ref, *rest, part
):
    out_ref, xs, ps, ls = rest[-4:]
    tok, width = v_ref.shape
    modes = dec_ref.shape[0]
    nb = tok // ROWS
    co = at_ref[0]
    own_half = co == part

    def chunk(j, carry):
        c = pl.ds(pl.multiple_of(j * LANES, LANES), LANES)
        base = pl.multiple_of(j * 2 * modes * nb, 2 * modes * nb)
        xs[...] = v_ref[:, c].astype(F32)
        chip = jnp.where(own_half, own_ref[0, :, c], theirs_ref[0, :, c])
        inner = other_ref[0:modes, c] + jnp.exp(-float(tok) * dec_ref[:, c]) * chip
        entering = jnp.where(co == 0, chip, inner)
        filter_chunk(xs, ps, ls, h_ref, s_ref, dec_ref, coef_ref, c, base, False, modes, nb, entering)
        out_ref[:, c] = o_ref[:, c].astype(F32) * xs[...]
        return carry

    lax.fori_loop(0, width // LANES, chunk, 0)


def lane_blocks(rows, width):
    return pl.BlockSpec((rows, width), lambda j: (0, j))


def local_states(v, g, o, decay, width):
    tok, ch = v.shape
    modes = decay.shape[0]
    srows = 2 * modes * (tok // ROWS)
    per = width // LANES * srows
    return pl.pallas_call(
        states_kernel,
        grid=(ch // width,),
        in_specs=[lane_blocks(tok, width)] * 3 + [lane_blocks(modes, width)],
        out_specs=[pl.BlockSpec((per, LANES), lambda j: (j, 0)), lane_blocks(2 * modes, width)],
        out_shape=[pltpu.VMEM((ch // LANES * srows, LANES), F32), pltpu.VMEM((2 * modes, ch), F32)],
        scratch_shapes=[pltpu.VMEM((tok, LANES), F32), pltpu.VMEM((tok, LANES), F32), pltpu.VMEM((modes, LANES), F32)],
        compiler_params=params(),
        name="states",
    )(*far([v, g, o, decay]))


def filter_scratch(tok, modes):
    return [
        pltpu.VMEM((tok, LANES), F32),
        pltpu.VMEM((modes * (tok // ROWS), LANES), F32),
        pltpu.VMEM((modes, LANES), F32),
    ]


def value_grad_half(at, mine, g, o, decay, coef, h, s, other, entry, width):
    tok, ch = g.shape
    modes = decay.shape[0]
    per = width // LANES * 2 * modes * (tok // ROWS)
    steps = ch // 2 // width

    def place(j, at):
        return (at[0] if mine else 1 - at[0]) * steps + j

    def cols(rows):
        return pl.BlockSpec((rows, width), lambda j, at: (0, place(j, at)))

    return pl.pallas_call(
        value_grad_kernel,
        grid_spec=pltpu.PrefetchScalarGridSpec(
            num_scalar_prefetch=1,
            grid=(steps,),
            in_specs=[cols(tok)] * 2
            + [cols(modes)] * 2
            + [
                cols(ROWS),
                pl.BlockSpec((per, LANES), lambda j, at: (place(j, at), 0)),
                cols(2 * modes),
                pl.BlockSpec((2, modes, width), lambda j, at: (0, 0, j)),
            ],
            out_specs=pl.BlockSpec((tok, width), lambda j, at: (0, j)),
            scratch_shapes=filter_scratch(tok, modes),
        ),
        out_shape=jax.ShapeDtypeStruct((tok, ch // 2), BF16),
        compiler_params=params(),
    )(at, *far([g, o, decay]), *near([coef, h]), s, *near([other, entry]))


def gate_grad_half(at, part, before, v, o, decay, coef, h, s, other, own, theirs, width):
    tok, ch = v.shape
    modes = decay.shape[0]
    per = width // LANES * 2 * modes * (tok // ROWS)
    steps = ch // 2 // width

    def cols(rows):
        return pl.BlockSpec((rows, width), lambda j, at: (0, part * steps + j))

    entry = pl.BlockSpec((2, modes, width), lambda j, at: (0, 0, j))
    args = [at, *far([v, o, decay]), *near([coef, h]), s, *near([other]), *far([own, theirs])]
    specs = [cols(tok)] * 2 + [cols(modes)] * 2
    specs += [cols(ROWS), pl.BlockSpec((per, LANES), lambda j, at: (part * steps + j, 0)), cols(2 * modes), entry, entry]
    aliases = {}
    if before is not None:
        aliases = {len(args): 0}
        args.append(before)
        specs.append(pl.BlockSpec(memory_space=pl.ANY))
    return pl.pallas_call(
        functools.partial(gate_grad_kernel, part=part),
        grid_spec=pltpu.PrefetchScalarGridSpec(
            num_scalar_prefetch=1,
            grid=(steps,),
            in_specs=specs,
            out_specs=cols(tok),
            scratch_shapes=filter_scratch(tok, modes),
        ),
        out_shape=jax.ShapeDtypeStruct((tok, ch), F32),
        input_output_aliases=aliases,
        compiler_params=params(),
    )(*args)


def combine_kernel(at_ref, st_ref, other_ref, dec_ref, *outs, tok):
    co, zl = at_ref[0], at_ref[4]
    modes, half = outs[0].shape
    c = pl.ds(pl.multiple_of(co * half, half), half)
    first = jnp.where(co == 0, st_ref[:, c], other_ref[:, c])
    second = jnp.where(co == 0, other_ref[:, c], st_ref[:, c])
    span = jnp.exp(-tok * dec_ref[:, c])
    chip_f = second[0:modes] + span * first[0:modes]
    chip_b = first[modes:] + span * second[modes:]
    for d in range(1, RING):
        outs[d - 1][...] = jnp.where(zl + d < RING, chip_f, chip_b)


def combine(at, st, other, decay, tok):
    modes, ch = decay.shape
    return pl.pallas_call(
        functools.partial(combine_kernel, tok=tok),
        in_specs=[smem()] + [vmem()] * 3,
        out_specs=[vmem()] * (RING - 1),
        out_shape=[pltpu.VMEM((modes, ch // 2), F32)] * (RING - 1),
        compiler_params=params(),
        name="combine",
    )(at, *near([st, other]), *far([decay]))


def enter_kernel(at_ref, dec_ref, *refs, tok):
    got, out = refs[:-1], refs[-1]
    co, zl = at_ref[0], at_ref[4]
    _, modes, half = out.shape
    decay = dec_ref[:, pl.ds(pl.multiple_of(co * half, half), half)]
    f = jnp.zeros((modes, half), F32)
    b = jnp.zeros((modes, half), F32)
    for d in range(1, RING):
        piece = got[d - 1][...]
        f = f + jnp.where(zl >= d, jnp.exp(-(2.0 * tok * (d - 1)) * decay) * piece, 0.0)
        b = b + jnp.where(zl < d, jnp.exp(-(2.0 * tok * (RING - 1 - d)) * decay) * piece, 0.0)
    out[0] = f
    out[1] = b


def enter(at, decay, got, tok):
    modes, ch = decay.shape
    return pl.pallas_call(
        functools.partial(enter_kernel, tok=tok),
        in_specs=[smem()] + [vmem()] * RING,
        out_specs=vmem(),
        out_shape=pltpu.VMEM((2, modes, ch // 2), F32),
        compiler_params=params(),
        name="enter",
    )(at, *far([decay]), *near(got))


def smem():
    return pl.BlockSpec(memory_space=pltpu.SMEM)


def vmem():
    return pl.BlockSpec(memory_space=pltpu.VMEM)


def pack_kernel(at_ref, own_ref, other_ref, *refs):
    outs, scr = refs[:RING], refs[RING]
    co, u = at_ref[0], at_ref[1]
    _, feat = own_ref.shape
    nzh = 2
    strip = feat // (nzh * RING)
    blk = strip // RING
    for k, src in enumerate((own_ref, other_ref)):

        @pl.when(co == 0)
        def _():
            for y in range(RING):
                for zh in range(nzh):
                    scr[y, k, :, zh * strip : (zh + 1) * strip] = src[:, (zh * RING + y) * strip : (zh * RING + y + 1) * strip]

        @pl.when(co == 1)
        def _():
            for x in range(RING):
                for zh in range(nzh):
                    parts = [
                        src[:, (zh * RING + y) * strip + x * blk : (zh * RING + y) * strip + (x + 1) * blk]
                        for y in range(RING)
                    ]
                    scr[x, k, :, zh * strip : (zh + 1) * strip] = jnp.concatenate(parts, axis=1)

    for d in range(RING):
        outs[d][...] = scr[(u + d) % RING]


def pack_inputs(at, own, other):
    tok, feat = own.shape
    piece = (2, tok, feat // RING)
    return pl.pallas_call(
        pack_kernel,
        in_specs=[smem(), vmem(), vmem()],
        out_specs=[vmem()] * RING,
        out_shape=[pltpu.VMEM(piece, BF16)] * RING,
        scratch_shapes=[pltpu.VMEM((RING,) + piece, BF16)],
        compiler_params=params(),
        name="pack_inputs",
    )(at, *far([own]), *near([other]))


def weight_part_kernel(at_ref, *refs):
    ins, grads = refs[:RING], refs[RING : 3 * RING]
    own, outs, pscr = refs[3 * RING], refs[3 * RING + 1 : 4 * RING], refs[4 * RING]
    w_at = at_ref[2]
    rows = jnp.concatenate([ins[d][k] for d in range(RING) for k in range(2)], axis=0)
    cols = jnp.concatenate([ref[...] for ref in grads], axis=0)
    part = lax.dot_general(rows, cols, (((0,), (0,)), ((), ())), preferred_element_type=F32)
    nzh, blk, _ = own.shape
    for zh in range(nzh):
        for w in range(RING):
            at = (zh * RING + w) * blk
            pscr[w, zh] = part[at : at + blk, :]
    own[...] = pscr[w_at]
    for d in range(1, RING):
        outs[d - 1][...] = pscr[(w_at + d) % RING].astype(BF16)


def weight_part(at, ins, grads):
    _, _, rows = ins[0].shape
    half = grads[0].shape[1]
    piece = (2, rows // (2 * RING), half)
    return pl.pallas_call(
        weight_part_kernel,
        in_specs=[smem()] + [vmem()] * (3 * RING),
        out_specs=[vmem()] * RING,
        out_shape=[pltpu.VMEM(piece, F32)] + [pltpu.VMEM(piece, BF16)] * (RING - 1),
        scratch_shapes=[pltpu.VMEM((RING,) + piece, F32)],
        compiler_params=params(),
        name="weight_part",
    )(at, *near(ins), *near(grads))


def input_part_kernel(at_ref, *refs):
    ws, grads, outs, wscr = refs[:RING], refs[RING : 3 * RING], refs[3 * RING : 4 * RING], refs[4 * RING]
    w_at, zh_at = at_ref[2], at_ref[3]
    tok = grads[0].shape[0]
    nzh, blk, _ = ws[0].shape
    for d in range(RING):
        for k in range(nzh):
            zh = (zh_at + k) % nzh
            w = (w_at + RING - d) % RING
            wscr[pl.ds(pl.multiple_of((zh * RING + w) * blk, blk), blk), :] = ws[d][k]
    rows = jnp.concatenate([ref[...] for ref in grads], axis=0)
    part = lax.dot_general(rows, wscr[...], (((1,), (1,)), ((), ())), preferred_element_type=F32)
    for d in range(RING):
        for k in range(2):
            at = (2 * d + k) * tok
            outs[d][k] = part[at : at + tok, :].astype(BF16)


def input_part(at, ws, grads):
    nzh, blk, half = ws[0].shape
    tok = grads[0].shape[0]
    rows = nzh * RING * blk
    return pl.pallas_call(
        input_part_kernel,
        in_specs=[smem()] + [vmem()] * (3 * RING),
        out_specs=[vmem()] * RING,
        out_shape=[pltpu.VMEM((2, tok, rows), BF16)] * RING,
        scratch_shapes=[pltpu.VMEM((rows, half), BF16)],
        compiler_params=params(),
        name="input_part",
    )(at, *near(ws), *far(grads))


def stack_kernel(*refs):
    for i, ref in enumerate(refs[:-1]):
        refs[-1][i] = ref[...]


def stack(parts):
    return pl.pallas_call(
        stack_kernel,
        in_specs=[vmem()] * len(parts),
        out_specs=vmem(),
        out_shape=pltpu.VMEM((len(parts),) + parts[0].shape, parts[0].dtype),
        compiler_params=params(),
        name="stack",
    )(*near(parts))


def pick_kernel(*refs):
    for i, ref in enumerate(refs[:-1]):
        refs[-1][i] = ref[1]


def pick_other(parts):
    return pl.pallas_call(
        pick_kernel,
        in_specs=[vmem()] * len(parts),
        out_specs=vmem(),
        out_shape=pltpu.VMEM((len(parts),) + parts[0].shape[1:], parts[0].dtype),
        compiler_params=params(),
        name="pick_other",
    )(*near(parts))


def ring_sum_kernel(at_ref, *refs, norm):
    parts, own, outs, scr = refs[:RING], refs[RING], refs[RING + 1 : -1], refs[-1]
    zl_at = at_ref[4]
    total = parts[0][...]
    for d in range(1, RING):
        total = total + parts[d][...].astype(F32)
    total = norm * total
    quarter = scr.shape[-1]
    for zl in range(RING):
        scr[zl] = total[:, :, zl * quarter : (zl + 1) * quarter]
    own[...] = scr[zl_at]
    for d in range(1, RING):
        outs[d - 1][...] = scr[(zl_at + d) % RING].astype(BF16)


def ring_sum(at, parts, norm):
    nzh, blk, half = parts[0].shape
    piece = (nzh, blk, half // RING)
    return pl.pallas_call(
        functools.partial(ring_sum_kernel, norm=norm),
        in_specs=[smem()] + [vmem()] * RING,
        out_specs=[vmem()] * RING,
        out_shape=[pltpu.VMEM(piece, F32)] + [pltpu.VMEM(piece, BF16)] * (RING - 1),
        scratch_shapes=[pltpu.VMEM((RING,) + piece, F32)],
        compiler_params=params(),
        name="ring_sum",
    )(at, *near(parts))


def line_sum_kernel(at_ref, *refs):
    parts, keep, send, scr = refs[:RING], refs[RING], refs[RING + 1], refs[RING + 2]
    total = parts[0][...]
    for ref in parts[1:]:
        total = total + ref[...].astype(F32)
    scr[...] = total
    keep[...] = scr[at_ref[3]]
    send[...] = scr[1 - at_ref[3]]


def line_sum(at, parts):
    shape = parts[0].shape
    return pl.pallas_call(
        line_sum_kernel,
        in_specs=[smem()] + [vmem()] * RING,
        out_specs=[vmem()] * 2,
        out_shape=[pltpu.VMEM(shape[1:], F32)] * 2,
        scratch_shapes=[pltpu.VMEM(shape, F32)],
        compiler_params=params(),
        name="line_sum",
    )(at, *near(parts))


def pair_sum_kernel(a_ref, b_ref, out_ref):
    out_ref[...] = a_ref[...] + b_ref[...]


def pair_sum(a, b):
    return pl.pallas_call(
        pair_sum_kernel,
        in_specs=[vmem()] * 2,
        out_specs=vmem(),
        out_shape=pltpu.VMEM(a.shape, F32),
        compiler_params=params(),
        name="pair_sum",
    )(*near([a, b]))


def join_kernel(at_ref, *refs):
    own, theirs, out = refs[:RING], refs[RING : 2 * RING], refs[-1]
    co, zl = at_ref[0], at_ref[4]
    quarter = own[0].shape[1]
    for d in range(RING):
        at = (zl + RING - d) % RING
        out[:, pl.ds(pl.multiple_of((co * RING + at) * quarter, quarter), quarter)] = own[d][...]
        out[:, pl.ds(pl.multiple_of(((1 - co) * RING + at) * quarter, quarter), quarter)] = theirs[d][...]


def join(at, own, theirs):
    blk, quarter = own[0].shape
    return pl.pallas_call(
        join_kernel,
        in_specs=[smem()] + [vmem()] * (2 * RING),
        out_specs=vmem(),
        out_shape=jax.ShapeDtypeStruct((blk, 2 * RING * quarter), F32),
        compiler_params=params(),
        name="join",
    )(at, *near(own), *near(theirs))


def assemble_kernel(at_ref, *refs):
    own, other, out, scr = refs[:RING], refs[RING], refs[RING + 1], refs[RING + 2]
    co, u, w = at_ref[0], at_ref[1], at_ref[2]
    nzh = 2
    strip = own[0].shape[2] // nzh
    blk = strip // RING
    for d in range(RING):
        scr[co, (u + d) % RING] = own[d][0].astype(F32)
        scr[1 - co, (w + d) % RING] = other[d].astype(F32)
    for zh in range(nzh):
        for y in range(RING):
            rows = scr[0, y, :, zh * strip : (zh + 1) * strip]
            parts = [scr[1, x, :, zh * strip + y * blk : zh * strip + (y + 1) * blk] for x in range(RING)]
            at = (zh * RING + y) * strip
            out[:, at : at + strip] = rows + jnp.concatenate(parts, axis=1)


def assemble(at, own, other):
    _, tok, cols = own[0].shape
    return pl.pallas_call(
        assemble_kernel,
        in_specs=[smem()] + [vmem()] * (RING + 1),
        out_specs=vmem(),
        out_shape=jax.ShapeDtypeStruct((tok, RING * cols), F32),
        scratch_shapes=[pltpu.VMEM((2, RING, tok, cols), F32)],
        compiler_params=params(),
        name="assemble",
    )(at, *near(own), *near([other]))


RINGS = ("co", "y", "x")


def shift(a, distance, gather):
    pairs = []
    for co in range(2):
        for y in range(RING):
            for x in range(RING):
                if (co == 0) == gather:
                    to = (co, (y + distance) % RING, x)
                else:
                    to = (co, y, (x + distance) % RING)
                pairs.append(((co * RING + y) * RING + x, (to[0] * RING + to[1]) * RING + to[2]))
    return lax.ppermute(a, RINGS, pairs)


def swap_cores(a):
    return lax.ppermute(a, "co", [(0, 1), (1, 0)])


def along(a, axes, distance):
    n = lax.axis_size(axes)
    return lax.ppermute(a, axes, [(i, (i + distance) % n) for i in range(n)])


def cross(a, distance):
    pairs = []
    for co in range(2):
        for y in range(RING):
            for x in range(RING):
                if co == 1:
                    to = (0, (y + distance) % RING, x)
                else:
                    to = (1, y, (x + distance) % RING)
                pairs.append(((co * RING + y) * RING + x, (to[0] * RING + to[1]) * RING + to[2]))
    return lax.ppermute(a, RINGS, pairs)


def on_device(inputs, values, gating, out_grad, weight, decay, gain):
    return step(inputs[0], values[0], gating[0], out_grad[0], weight, decay, gain)


def step(inp, v, g, o, weight, decay, gain):
    tok, ch = v.shape
    nzl, nco, nzh, ny, nx = (lax.axis_size(a) for a in ("zl", "co", "zh", "y", "x"))
    co, zh, y, x, zl = (lax.axis_index(a).astype(jnp.int32) for a in ("co", "zh", "y", "x", "zl"))
    gather_at = jnp.where(co == 0, y, x)
    reduce_at = jnp.where(co == 0, x, y)
    at = jnp.stack([co, gather_at, reduce_at, zh, zl])
    half = ch // nco
    width = min(512, half)

    w_half = lax.dynamic_slice_in_dim(weight, co * half, half, axis=1)
    w_other = along(w_half, "zh", 1)
    w_pair = stack([w_half, w_other])
    inp_other = swap_cores(inp)

    s, st = local_states(v, g, o, decay, width)
    other = swap_cores(st)
    coef = gain * jnp.sqrt(-jnp.expm1(-2.0 * decay))
    lags = jnp.arange(ROWS, dtype=F32)
    h = jnp.sum(coef[None] * jnp.exp(-decay[None] * lags[:, None, None]), axis=1)
    send = combine(at, st, other, decay, float(tok))
    ends = []
    for d in range(1, RING):
        ends.append(along(send[d - 1], "zl", d))

    packed = pack_inputs(at, inp, inp_other)
    ins = [packed[0]]
    for d in range(1, RING):
        ins.append(shift(packed[d], d, True))
    ws = [w_pair]
    for d in range(1, RING):
        ws.append(shift(w_pair, d, False))

    own_in = enter(at, decay, ends, float(tok))
    their_in = swap_cores(own_in)
    own = value_grad_half(at, True, g, o, decay, coef, h, s, other, own_in, width)
    give = value_grad_half(at, False, g, o, decay, coef, h, s, other, their_in, width)
    grads = [own, None]
    for d in range(1, RING):
        grads.append(shift(own, d, True))
        grads.append(cross(give, d))
    grads[1] = cross(give, 0)
    gate_grad = None
    for part in range(2):
        gate_grad = gate_grad_half(
            at, part, gate_grad, v, o, decay, coef, h, s, other, own_in, their_in, width
        )

    parts = weight_part(at, ins, grads)
    norm = 1.0 / math.sqrt(tok * nzl * nco * nzh * ny * nx)
    sums = [parts[0]]
    for d in range(1, RING):
        sums.append(shift(parts[d], d, False))
    backs = list(input_part(at, ws, grads))
    for d in range(1, RING):
        backs[d] = shift(backs[d], -d, True)
    pieces = ring_sum(at, sums, norm)
    line = [pieces[0]]
    for d in range(1, RING):
        line.append(along(pieces[d], "zl", d))
    keep, send_zh = line_sum(at, line)
    got_zh = along(send_zh, "zh", 1)
    picked = pick_other(backs)
    theirs = swap_cores(picked)
    total = pair_sum(keep, got_zh)
    mine, rest = [total], []
    for d in range(1, nzl):
        mine.append(along(total, "zl", d))
    for d in range(nzl):
        rest.append(swap_cores(mine[d]))
    in_grad = assemble(at, backs, theirs)
    weight_grad = join(at, mine, rest)
    return (in_grad[None], gate_grad[None], weight_grad)


def solution(mesh):
    n_ctx, n_dp = mesh.devices.shape
    fine = Mesh(mesh.devices.reshape(n_ctx // 2, 2, n_dp // 16, 4, 4), CTX + DP)
    rows = P(DP, CTX, None)
    return jax.shard_map(
        on_device,
        mesh=fine,
        in_specs=(rows, rows, rows, rows, P(DP, None), P(), P()),
        out_specs=(rows, rows, P(DP, None)),
        check_vma=False,
    )
```

```python
import functools
import math

import jax
import jax.numpy as jnp
from jax import lax
from jax.experimental import pallas as pl
from jax.experimental.pallas import tpu as pltpu
from jax.sharding import Mesh, PartitionSpec as P


F32 = jnp.float32
BF16 = jnp.bfloat16
LANES = 128
ROWS = 16
RING = 4
CTX = ("zl", "co")
DP = ("zh", "y", "x")


def far(arrays):
    return [pltpu.with_memory_space_constraint(a, pltpu.HBM) for a in arrays]


def near(arrays):
    return [pltpu.with_memory_space_constraint(a, pltpu.VMEM) for a in arrays]


def params():
    return pltpu.CompilerParams(vmem_limit_bytes=24 * 1024 * 1024)


def states_kernel(v_ref, g_ref, o_ref, dec_ref, s_ref, st_ref, xs, us, ls):
    tok, width = v_ref.shape
    modes = dec_ref.shape[0]
    nb = tok // ROWS
    half = modes * nb

    def chunk(j, carry):
        c = pl.ds(pl.multiple_of(j * LANES, LANES), LANES)
        base = pl.multiple_of(j * 2 * half, 2 * half)
        decay = dec_ref[:, c]
        ls[...] = jnp.exp(-decay)
        d16 = jnp.exp(-float(ROWS) * decay)
        xs[...] = v_ref[:, c].astype(F32)
        us[...] = g_ref[:, c].astype(F32) * o_ref[:, c].astype(F32)
        x = [xs[pl.ds(r, nb, stride=ROWS), :] for r in range(ROWS)]
        u = [us[pl.ds(r, nb, stride=ROWS), :] for r in range(ROWS)]
        for m in range(modes):
            lam = jnp.broadcast_to(ls[pl.ds(m, 1), :], (nb, LANES))
            s = x[0]
            b = u[ROWS - 1]
            for r in range(1, ROWS):
                s = s * lam + x[r]
                b = b * lam + u[ROWS - 1 - r]
            s_ref[pl.ds(base + m * nb, nb), :] = s
            s_ref[pl.ds(base + half + m * nb, nb), :] = b
        f = s_ref[pl.ds(base, modes, stride=nb), :]
        b = s_ref[pl.ds(base + half + nb - 1, modes, stride=nb), :]
        for i in range(1, nb):
            f = f * d16 + s_ref[pl.ds(base + i, modes, stride=nb), :]
            b = b * d16 + s_ref[pl.ds(base + half + nb - 1 - i, modes, stride=nb), :]
        st_ref[0:modes, c] = f
        st_ref[modes : 2 * modes, c] = b
        return carry

    lax.fori_loop(0, width // LANES, chunk, 0)


def filter_chunk(src, ps, ls, h_ref, s_ref, dec_ref, coef_ref, c, base, back, modes, nb, entering):
    decay = dec_ref[:, c]
    ls[...] = jnp.exp(-decay)
    d16 = jnp.exp(-float(ROWS) * decay)
    coef = coef_ref[:, c]
    p = entering
    for i in range(nb):
        at = nb - 1 - i if back else i
        ps[pl.ds(at, modes, stride=nb), :] = p * coef
        if i < nb - 1:
            p = p * d16 + s_ref[pl.ds(base + (modes * nb if back else 0) + at, modes, stride=nb), :]
    order = list(range(ROWS))
    if back:
        order = order[::-1]
    x = [src[pl.ds(r, nb, stride=ROWS), :] for r in order]
    y = [None] * ROWS
    for lag in range(ROWS):
        h = jnp.broadcast_to(h_ref[pl.ds(lag, 1), c], (nb, LANES))
        for r in range(lag, ROWS):
            term = h * x[r - lag]
            y[r] = term if lag == 0 else y[r] + term
    for m in range(modes):
        lam = jnp.broadcast_to(ls[pl.ds(m, 1), :], (nb, LANES))
        q = ps[pl.ds(m * nb, nb), :]
        for r in range(ROWS):
            q = q * lam
            y[r] = y[r] + q
    for i, r in enumerate(order):
        src[pl.ds(r, nb, stride=ROWS), :] = y[i]


def value_grad_kernel(at_ref, g_ref, o_ref, dec_ref, coef_ref, h_ref, s_ref, other_ref, in_ref, out_ref, us, ps, ls):
    tok, width = g_ref.shape
    modes = dec_ref.shape[0]
    nb = tok // ROWS
    co = at_ref[0]

    def chunk(j, carry):
        c = pl.ds(pl.multiple_of(j * LANES, LANES), LANES)
        base = pl.multiple_of(j * 2 * modes * nb, 2 * modes * nb)
        us[...] = g_ref[:, c].astype(F32) * o_ref[:, c].astype(F32)
        chip = in_ref[1, :, c]
        inner = other_ref[modes : 2 * modes, c] + jnp.exp(-float(tok) * dec_ref[:, c]) * chip
        entering = jnp.where(co == 1, chip, inner)
        filter_chunk(us, ps, ls, h_ref, s_ref, dec_ref, coef_ref, c, base, True, modes, nb, entering)
        out_ref[:, c] = us[...].astype(BF16)
        return carry

    lax.fori_loop(0, width // LANES, chunk, 0)


def gate_grad_kernel(
    at_ref, v_ref, o_ref, dec_ref, coef_ref, h_ref, s_ref, other_ref, own_ref, theirs_ref, out_ref, xs, ps, ls
):
    tok, width = v_ref.shape
    modes = dec_ref.shape[0]
    nb = tok // ROWS
    co = at_ref[0]
    own_half = pl.program_id(0) // (pl.num_programs(0) // 2) == co

    def chunk(j, carry):
        c = pl.ds(pl.multiple_of(j * LANES, LANES), LANES)
        base = pl.multiple_of(j * 2 * modes * nb, 2 * modes * nb)
        xs[...] = v_ref[:, c].astype(F32)
        chip = jnp.where(own_half, own_ref[0, :, c], theirs_ref[0, :, c])
        inner = other_ref[0:modes, c] + jnp.exp(-float(tok) * dec_ref[:, c]) * chip
        entering = jnp.where(co == 0, chip, inner)
        filter_chunk(xs, ps, ls, h_ref, s_ref, dec_ref, coef_ref, c, base, False, modes, nb, entering)
        out_ref[:, c] = o_ref[:, c].astype(F32) * xs[...]
        return carry

    lax.fori_loop(0, width // LANES, chunk, 0)


def lane_blocks(rows, width):
    return pl.BlockSpec((rows, width), lambda j: (0, j))


def local_states(v, g, o, decay, width):
    tok, ch = v.shape
    modes = decay.shape[0]
    srows = 2 * modes * (tok // ROWS)
    per = width // LANES * srows
    return pl.pallas_call(
        states_kernel,
        grid=(ch // width,),
        in_specs=[lane_blocks(tok, width)] * 3 + [lane_blocks(modes, width)],
        out_specs=[pl.BlockSpec((per, LANES), lambda j: (j, 0)), lane_blocks(2 * modes, width)],
        out_shape=[pltpu.VMEM((ch // LANES * srows, LANES), F32), pltpu.VMEM((2 * modes, ch), F32)],
        scratch_shapes=[pltpu.VMEM((tok, LANES), F32), pltpu.VMEM((tok, LANES), F32), pltpu.VMEM((modes, LANES), F32)],
        compiler_params=params(),
        name="states",
    )(*far([v, g, o, decay]))


def filter_scratch(tok, modes):
    return [
        pltpu.VMEM((tok, LANES), F32),
        pltpu.VMEM((modes * (tok // ROWS), LANES), F32),
        pltpu.VMEM((modes, LANES), F32),
    ]


def value_grad_half(at, mine, g, o, decay, coef, h, s, other, entry, width):
    tok, ch = g.shape
    modes = decay.shape[0]
    per = width // LANES * 2 * modes * (tok // ROWS)
    steps = ch // 2 // width

    def place(j, at):
        return (at[0] if mine else 1 - at[0]) * steps + j

    def cols(rows):
        return pl.BlockSpec((rows, width), lambda j, at: (0, place(j, at)))

    return pl.pallas_call(
        value_grad_kernel,
        grid_spec=pltpu.PrefetchScalarGridSpec(
            num_scalar_prefetch=1,
            grid=(steps,),
            in_specs=[cols(tok)] * 2
            + [cols(modes)] * 2
            + [
                cols(ROWS),
                pl.BlockSpec((per, LANES), lambda j, at: (place(j, at), 0)),
                cols(2 * modes),
                pl.BlockSpec((2, modes, width), lambda j, at: (0, 0, j)),
            ],
            out_specs=pl.BlockSpec((tok, width), lambda j, at: (0, j)),
            scratch_shapes=filter_scratch(tok, modes),
        ),
        out_shape=jax.ShapeDtypeStruct((tok, ch // 2), BF16),
        compiler_params=params(),
    )(at, *far([g, o, decay]), *near([coef, h]), s, *near([other, entry]))


def local_gate_grad(at, v, o, decay, coef, h, s, other, own, theirs, width):
    tok, ch = v.shape
    modes = decay.shape[0]
    per = width // LANES * 2 * modes * (tok // ROWS)
    steps = ch // 2 // width

    def cols(rows):
        return pl.BlockSpec((rows, width), lambda j, at: (0, j))

    entry = pl.BlockSpec((2, modes, width), lambda j, at: (0, 0, j % steps))
    return pl.pallas_call(
        gate_grad_kernel,
        grid_spec=pltpu.PrefetchScalarGridSpec(
            num_scalar_prefetch=1,
            grid=(2 * steps,),
            in_specs=[cols(tok)] * 2
            + [cols(modes)] * 2
            + [cols(ROWS), pl.BlockSpec((per, LANES), lambda j, at: (j, 0)), cols(2 * modes), entry, entry],
            out_specs=cols(tok),
            scratch_shapes=filter_scratch(tok, modes),
        ),
        out_shape=jax.ShapeDtypeStruct((tok, ch), F32),
        compiler_params=params(),
        name="gate_grad",
    )(at, *far([v, o, decay]), *near([coef, h]), s, *near([other]), *far([own, theirs]))


def combine_kernel(at_ref, st_ref, other_ref, dec_ref, *outs, tok):
    co, zl = at_ref[0], at_ref[4]
    modes, half = outs[0].shape
    c = pl.ds(pl.multiple_of(co * half, half), half)
    first = jnp.where(co == 0, st_ref[:, c], other_ref[:, c])
    second = jnp.where(co == 0, other_ref[:, c], st_ref[:, c])
    span = jnp.exp(-tok * dec_ref[:, c])
    chip_f = second[0:modes] + span * first[0:modes]
    chip_b = first[modes:] + span * second[modes:]
    for d in range(1, RING):
        outs[d - 1][...] = jnp.where(zl + d < RING, chip_f, chip_b)


def combine(at, st, other, decay, tok):
    modes, ch = decay.shape
    return pl.pallas_call(
        functools.partial(combine_kernel, tok=tok),
        in_specs=[smem()] + [vmem()] * 3,
        out_specs=[vmem()] * (RING - 1),
        out_shape=[pltpu.VMEM((modes, ch // 2), F32)] * (RING - 1),
        compiler_params=params(),
        name="combine",
    )(at, *near([st, other]), *far([decay]))


def enter_kernel(at_ref, dec_ref, *refs, tok):
    got, out = refs[:-1], refs[-1]
    co, zl = at_ref[0], at_ref[4]
    _, modes, half = out.shape
    decay = dec_ref[:, pl.ds(pl.multiple_of(co * half, half), half)]
    f = jnp.zeros((modes, half), F32)
    b = jnp.zeros((modes, half), F32)
    for d in range(1, RING):
        piece = got[d - 1][...]
        f = f + jnp.where(zl >= d, jnp.exp(-(2.0 * tok * (d - 1)) * decay) * piece, 0.0)
        b = b + jnp.where(zl < d, jnp.exp(-(2.0 * tok * (RING - 1 - d)) * decay) * piece, 0.0)
    out[0] = f
    out[1] = b


def enter(at, decay, got, tok):
    modes, ch = decay.shape
    return pl.pallas_call(
        functools.partial(enter_kernel, tok=tok),
        in_specs=[smem()] + [vmem()] * RING,
        out_specs=vmem(),
        out_shape=pltpu.VMEM((2, modes, ch // 2), F32),
        compiler_params=params(),
        name="enter",
    )(at, *far([decay]), *near(got))


def smem():
    return pl.BlockSpec(memory_space=pltpu.SMEM)


def vmem():
    return pl.BlockSpec(memory_space=pltpu.VMEM)


def pack_kernel(at_ref, own_ref, other_ref, *refs):
    outs, scr = refs[:RING], refs[RING]
    co, u = at_ref[0], at_ref[1]
    _, feat = own_ref.shape
    nzh = 2
    strip = feat // (nzh * RING)
    blk = strip // RING
    for k, src in enumerate((own_ref, other_ref)):

        @pl.when(co == 0)
        def _():
            for y in range(RING):
                for zh in range(nzh):
                    scr[y, k, :, zh * strip : (zh + 1) * strip] = src[:, (zh * RING + y) * strip : (zh * RING + y + 1) * strip]

        @pl.when(co == 1)
        def _():
            for x in range(RING):
                for zh in range(nzh):
                    parts = [
                        src[:, (zh * RING + y) * strip + x * blk : (zh * RING + y) * strip + (x + 1) * blk]
                        for y in range(RING)
                    ]
                    scr[x, k, :, zh * strip : (zh + 1) * strip] = jnp.concatenate(parts, axis=1)

    for d in range(RING):
        outs[d][...] = scr[(u + d) % RING]


def pack_inputs(at, own, other):
    tok, feat = own.shape
    piece = (2, tok, feat // RING)
    return pl.pallas_call(
        pack_kernel,
        in_specs=[smem(), vmem(), vmem()],
        out_specs=[vmem()] * RING,
        out_shape=[pltpu.VMEM(piece, BF16)] * RING,
        scratch_shapes=[pltpu.VMEM((RING,) + piece, BF16)],
        compiler_params=params(),
        name="pack_inputs",
    )(at, *far([own]), *near([other]))


def weight_part_kernel(at_ref, *refs):
    ins, grads = refs[:RING], refs[RING : 3 * RING]
    own, outs, pscr = refs[3 * RING], refs[3 * RING + 1 : 4 * RING], refs[4 * RING]
    w_at = at_ref[2]
    rows = jnp.concatenate([ins[d][k] for d in range(RING) for k in range(2)], axis=0)
    cols = jnp.concatenate([ref[...] for ref in grads], axis=0)
    part = lax.dot_general(rows, cols, (((0,), (0,)), ((), ())), preferred_element_type=F32)
    nzh, blk, _ = own.shape
    for zh in range(nzh):
        for w in range(RING):
            at = (zh * RING + w) * blk
            pscr[w, zh] = part[at : at + blk, :]
    own[...] = pscr[w_at]
    for d in range(1, RING):
        outs[d - 1][...] = pscr[(w_at + d) % RING].astype(BF16)


def weight_part(at, ins, grads):
    _, _, rows = ins[0].shape
    half = grads[0].shape[1]
    piece = (2, rows // (2 * RING), half)
    return pl.pallas_call(
        weight_part_kernel,
        in_specs=[smem()] + [vmem()] * (3 * RING),
        out_specs=[vmem()] * RING,
        out_shape=[pltpu.VMEM(piece, F32)] + [pltpu.VMEM(piece, BF16)] * (RING - 1),
        scratch_shapes=[pltpu.VMEM((RING,) + piece, F32)],
        compiler_params=params(),
        name="weight_part",
    )(at, *near(ins), *near(grads))


def input_part_kernel(at_ref, *refs):
    ws, grads, outs, wscr = refs[:RING], refs[RING : 3 * RING], refs[3 * RING : 4 * RING], refs[4 * RING]
    w_at, zh_at = at_ref[2], at_ref[3]
    tok = grads[0].shape[0]
    nzh, blk, _ = ws[0].shape
    for d in range(RING):
        for k in range(nzh):
            zh = (zh_at + k) % nzh
            w = (w_at + RING - d) % RING
            wscr[pl.ds(pl.multiple_of((zh * RING + w) * blk, blk), blk), :] = ws[d][k]
    rows = jnp.concatenate([ref[...] for ref in grads], axis=0)
    part = lax.dot_general(rows, wscr[...], (((1,), (1,)), ((), ())), preferred_element_type=F32)
    for d in range(RING):
        for k in range(2):
            at = (2 * d + k) * tok
            outs[d][k] = part[at : at + tok, :].astype(BF16)


def input_part(at, ws, grads):
    nzh, blk, half = ws[0].shape
    tok = grads[0].shape[0]
    rows = nzh * RING * blk
    return pl.pallas_call(
        input_part_kernel,
        in_specs=[smem()] + [vmem()] * (3 * RING),
        out_specs=[vmem()] * RING,
        out_shape=[pltpu.VMEM((2, tok, rows), BF16)] * RING,
        scratch_shapes=[pltpu.VMEM((rows, half), BF16)],
        compiler_params=params(),
        name="input_part",
    )(at, *near(ws), *far(grads))


def stack_kernel(*refs):
    for i, ref in enumerate(refs[:-1]):
        refs[-1][i] = ref[...]


def stack(parts):
    return pl.pallas_call(
        stack_kernel,
        in_specs=[vmem()] * len(parts),
        out_specs=vmem(),
        out_shape=pltpu.VMEM((len(parts),) + parts[0].shape, parts[0].dtype),
        compiler_params=params(),
        name="stack",
    )(*near(parts))


def pick_kernel(*refs):
    for i, ref in enumerate(refs[:-1]):
        refs[-1][i] = ref[1]


def pick_other(parts):
    return pl.pallas_call(
        pick_kernel,
        in_specs=[vmem()] * len(parts),
        out_specs=vmem(),
        out_shape=pltpu.VMEM((len(parts),) + parts[0].shape[1:], parts[0].dtype),
        compiler_params=params(),
        name="pick_other",
    )(*near(parts))


def ring_sum_kernel(at_ref, *refs, norm):
    parts, own, out, scr = refs[:RING], refs[RING], refs[RING + 1], refs[RING + 2]
    total = parts[0][...]
    for d in range(1, RING):
        total = total + parts[d][...].astype(F32)
    total = norm * total
    n, _, quarter = scr.shape
    for zh in range(n // RING):
        for zl in range(RING):
            scr[zh * RING + zl] = total[zh, :, zl * quarter : (zl + 1) * quarter]
    own[...] = scr[at_ref[3] * RING + at_ref[4]]
    out[...] = scr[...].astype(BF16)


def ring_sum(at, parts, norm):
    nzh, blk, half = parts[0].shape
    n = nzh * RING
    piece = (blk, half // RING)
    return pl.pallas_call(
        functools.partial(ring_sum_kernel, norm=norm),
        in_specs=[smem()] + [vmem()] * RING,
        out_specs=[vmem()] * 2,
        out_shape=[pltpu.VMEM(piece, F32), pltpu.VMEM((n,) + piece, BF16)],
        scratch_shapes=[pltpu.VMEM((n,) + piece, F32)],
        compiler_params=params(),
        name="ring_sum",
    )(at, *near(parts))


def line_sum_kernel(at_ref, own_ref, got_ref, out_ref):
    z = at_ref[3] * RING + at_ref[4]
    total = own_ref[...]
    for i in range(got_ref.shape[0]):
        total = total + jnp.where(z == i, 0.0, got_ref[i].astype(F32))
    out_ref[...] = total


def line_sum(at, own, got):
    return pl.pallas_call(
        line_sum_kernel,
        in_specs=[smem()] + [vmem()] * 2,
        out_specs=vmem(),
        out_shape=pltpu.VMEM(own.shape, F32),
        compiler_params=params(),
        name="line_sum",
    )(at, *near([own, got]))


def join_kernel(at_ref, *refs):
    own, theirs, out = refs[:RING], refs[RING : 2 * RING], refs[-1]
    co, zl = at_ref[0], at_ref[4]
    quarter = own[0].shape[1]
    for d in range(RING):
        at = (zl + RING - d) % RING
        out[:, pl.ds(pl.multiple_of((co * RING + at) * quarter, quarter), quarter)] = own[d][...]
        out[:, pl.ds(pl.multiple_of(((1 - co) * RING + at) * quarter, quarter), quarter)] = theirs[d][...]


def join(at, own, theirs):
    blk, quarter = own[0].shape
    return pl.pallas_call(
        join_kernel,
        in_specs=[smem()] + [vmem()] * (2 * RING),
        out_specs=vmem(),
        out_shape=jax.ShapeDtypeStruct((blk, 2 * RING * quarter), F32),
        compiler_params=params(),
        name="join",
    )(at, *near(own), *near(theirs))


def assemble_kernel(at_ref, *refs):
    own, other, out, scr = refs[:RING], refs[RING], refs[RING + 1], refs[RING + 2]
    co, u, w = at_ref[0], at_ref[1], at_ref[2]
    nzh = 2
    strip = own[0].shape[2] // nzh
    blk = strip // RING
    for d in range(RING):
        scr[co, (u + d) % RING] = own[d][0].astype(F32)
        scr[1 - co, (w + d) % RING] = other[d].astype(F32)
    for zh in range(nzh):
        for y in range(RING):
            rows = scr[0, y, :, zh * strip : (zh + 1) * strip]
            parts = [scr[1, x, :, zh * strip + y * blk : zh * strip + (y + 1) * blk] for x in range(RING)]
            at = (zh * RING + y) * strip
            out[:, at : at + strip] = rows + jnp.concatenate(parts, axis=1)


def assemble(at, own, other):
    _, tok, cols = own[0].shape
    return pl.pallas_call(
        assemble_kernel,
        in_specs=[smem()] + [vmem()] * (RING + 1),
        out_specs=vmem(),
        out_shape=jax.ShapeDtypeStruct((tok, RING * cols), F32),
        scratch_shapes=[pltpu.VMEM((2, RING, tok, cols), F32)],
        compiler_params=params(),
        name="assemble",
    )(at, *near(own), *near([other]))


RINGS = ("co", "y", "x")


def shift(a, distance, gather):
    pairs = []
    for co in range(2):
        for y in range(RING):
            for x in range(RING):
                if (co == 0) == gather:
                    to = (co, (y + distance) % RING, x)
                else:
                    to = (co, y, (x + distance) % RING)
                pairs.append(((co * RING + y) * RING + x, (to[0] * RING + to[1]) * RING + to[2]))
    return lax.ppermute(a, RINGS, pairs)


def swap_cores(a):
    return lax.ppermute(a, "co", [(0, 1), (1, 0)])


def along(a, axes, distance):
    n = lax.axis_size(axes)
    return lax.ppermute(a, axes, [(i, (i + distance) % n) for i in range(n)])


def cross(a, distance):
    pairs = []
    for co in range(2):
        for y in range(RING):
            for x in range(RING):
                if co == 1:
                    to = (0, (y + distance) % RING, x)
                else:
                    to = (1, y, (x + distance) % RING)
                pairs.append(((co * RING + y) * RING + x, (to[0] * RING + to[1]) * RING + to[2]))
    return lax.ppermute(a, RINGS, pairs)


def on_device(inputs, values, gating, out_grad, weight, decay, gain):
    return step(inputs[0], values[0], gating[0], out_grad[0], weight, decay, gain)


def step(inp, v, g, o, weight, decay, gain):
    tok, ch = v.shape
    nzl, nco, nzh, ny, nx = (lax.axis_size(a) for a in ("zl", "co", "zh", "y", "x"))
    co, zh, y, x, zl = (lax.axis_index(a).astype(jnp.int32) for a in ("co", "zh", "y", "x", "zl"))
    gather_at = jnp.where(co == 0, y, x)
    reduce_at = jnp.where(co == 0, x, y)
    at = jnp.stack([co, gather_at, reduce_at, zh, zl])
    half = ch // nco
    width = min(512, half)

    w_half = lax.dynamic_slice_in_dim(weight, co * half, half, axis=1)
    w_other = along(w_half, "zh", 1)
    w_pair = stack([w_half, w_other])
    inp_other = swap_cores(inp)

    s, st = local_states(v, g, o, decay, width)
    other = swap_cores(st)
    coef = gain * jnp.sqrt(-jnp.expm1(-2.0 * decay))
    lags = jnp.arange(ROWS, dtype=F32)
    h = jnp.sum(coef[None] * jnp.exp(-decay[None] * lags[:, None, None]), axis=1)
    send = combine(at, st, other, decay, float(tok))
    ends = []
    for d in range(1, RING):
        ends.append(along(send[d - 1], "zl", d))

    packed = pack_inputs(at, inp, inp_other)
    ins = [packed[0]]
    for d in range(1, RING):
        ins.append(shift(packed[d], d, True))
    ws = [w_pair]
    for d in range(1, RING):
        ws.append(shift(w_pair, d, False))

    own_in = enter(at, decay, ends, float(tok))
    their_in = swap_cores(own_in)
    own = value_grad_half(at, True, g, o, decay, coef, h, s, other, own_in, width)
    give = value_grad_half(at, False, g, o, decay, coef, h, s, other, their_in, width)
    own1 = shift(own, 1, True)
    own3 = shift(own, RING - 1, True)
    own2 = shift(own1, 1, True)
    give0 = cross(give, 0)
    give1 = cross(give, 1)
    give3 = cross(give, RING - 1)
    give2 = shift(give3, RING - 1, True)
    grads = [own, give0, own1, give1, own2, give2, own3, give3]
    gate_grad = local_gate_grad(at, v, o, decay, coef, h, s, other, own_in, their_in, width)

    parts = weight_part(at, ins, grads)
    norm = 1.0 / math.sqrt(tok * nzl * nco * nzh * ny * nx)
    sums = [parts[0]]
    for d in range(1, RING):
        sums.append(shift(parts[d], d, False))
    backs = list(input_part(at, ws, grads))
    for d in range(1, RING):
        backs[d] = shift(backs[d], -d, True)
    pieces = ring_sum(at, sums, norm)
    got = lax.all_to_all(pieces[1], ("zh", "zl"), split_axis=0, concat_axis=0, tiled=True)
    picked = pick_other(backs)
    theirs = swap_cores(picked)
    total = line_sum(at, pieces[0], got)
    mine, rest = [total], []
    for d in range(1, nzl):
        mine.append(along(total, "zl", d))
    for d in range(nzl):
        rest.append(swap_cores(mine[d]))
    in_grad = assemble(at, backs, theirs)
    weight_grad = join(at, mine, rest)
    return (in_grad[None], gate_grad[None], weight_grad)


def solution(mesh):
    n_ctx, n_dp = mesh.devices.shape
    fine = Mesh(mesh.devices.reshape(n_ctx // 2, 2, n_dp // 16, 4, 4), CTX + DP)
    rows = P(DP, CTX, None)
    return jax.shard_map(
        on_device,
        mesh=fine,
        in_specs=(rows, rows, rows, rows, P(DP, None), P(), P()),
        out_specs=(rows, rows, P(DP, None)),
        check_vma=False,
    )
```
